128 devices in a mesh: contour: 4 (over x), clus: 32 (over y, z, core).
Axes of the slice: x: 4, y: 4, z: 4, core: 2. Of those that a mesh axis runs over, the one named last changes fastest.
Arguments:
- probes: float32 [256, 2, 16, 128], P('clus'), may hold values from -18 to 18
- near_blocks: bfloat16 [1024, 27, 2, 128, 128], P(('contour', 'clus')), parts along dimension 0
- near_list: int32 [256, 27], P('clus'), may hold values from 0 to 255, as said below
- near_count: int32 [256], P('clus'), may hold values from 1 to 27
- cluster_rows: int32 [256], P('clus'), may hold values from 64 to 128
- row_basis: bfloat16 [1024, 2, 32, 128], P(('contour', 'clus')), parts along dimension 0, may hold values from -1 to 1
- col_basis: bfloat16 [1024, 2, 32, 128], P(('contour', 'clus')), parts along dimension 0, may hold values from -0.5 to 0.5
- far_list: int32 [256, 32], P('clus'), may hold values from 0 to 255, as said below
- far_coupling: float32 [1024, 32, 2, 32, 32], P(('contour', 'clus')), parts along dimension 0, may hold values from -0.375 to 0.375
- weight: float32 [8], P('contour'), parts along dimension 0, may hold values from -6 to 6
Outputs:
- solution: float32 [1024, 2, 16, 128], P(('contour', 'clus')), parts along dimension 0
- moment: float32 [8, 16, 16], P('contour'), parts along dimension 0
- arnoldi: float32 [16, 16], P('contour'), parts along dimension 0
The draws below stay inside these ranges and needn't reach their ends.
There are 4 independent parts, one for each index of `contour`. The reference program is written for one: setup_inputs(seed, part) draws one part's arguments, and reference() takes and returns one part's arrays. A program takes and returns all parts, laid end to end along the dimension named above; an argument that names none is the same for every part. Nothing has to cross between parts.
Inputs may be any that keep to these rules, and one draw needn't show every extreme that they name: near_list[i, 0] = i; every entry lies within 8 clusters of i. `far_list`: every entry j of cluster i's list has min(|j - i|, 256 - |j - i|) > 8, so no far slot names a cluster of i's near list.
All inputs are finite; a program needn't handle non-finite values.
Results may differ from the reference program's by a relative error of at most 0.0019.
Values may be sent and summed in bfloat16 or wider, within the bound.
No kernel may reach another device: no remote copies, remote signals or barrier semaphores. Data moves between devices by JAX's collectives and lax.ppermute only.
A program may use at most 128 MiB of HBM per device.

```python
import jax
import jax.numpy as jnp
from jax import lax

BS = 128
RANK = 32
PROBES = 16
KMAX = 27
FMAX = 32
NB_DEV = 8
CLUSTERS = 256


def draw_probes(key, part):
    shape = (CLUSTERS, 2, PROBES, BS)
    place = lax.broadcasted_iota(jnp.int32, shape, 0).astype(jnp.float32) / (CLUSTERS - 1)
    noise = jnp.clip(jax.random.normal(key, shape, jnp.float32), -6.0, 6.0)
    values = noise * (1.0 + 2.0 * place)
    return values.astype(jnp.float32)


def draw_near_blocks(key, part):
    key_one, key_two, key_three = jax.random.split(key, 3)
    shape = (CLUSTERS, KMAX, 2, BS, BS)
    spread = 0.5 / (BS * KMAX) ** 0.5
    noise = jax.random.normal(key_one, shape, jnp.float32) * spread
    diag_re = jax.random.uniform(key_two, (CLUSTERS, BS), jnp.float32, 2.5, 3.5)
    diag_im = jax.random.uniform(key_three, (CLUSTERS, BS), jnp.float32, -1.0, 1.0)
    eye = (lax.broadcasted_iota(jnp.int32, (BS, BS), 0) == lax.broadcasted_iota(jnp.int32, (BS, BS), 1)).astype(jnp.float32)
    noise = noise.at[:, 0, 0].add(diag_re[:, :, None] * eye[None])
    noise = noise.at[:, 0, 1].add(diag_im[:, :, None] * eye[None])
    return noise.astype(jnp.bfloat16)


def draw_near_list(key, part):
    offsets = jax.random.randint(key, (CLUSTERS, KMAX), -NB_DEV, NB_DEV + 1)
    offsets = offsets.at[:, 0].set(0)
    base = lax.broadcasted_iota(jnp.int32, (CLUSTERS, KMAX), 0)
    return jnp.clip(base + offsets, 0, CLUSTERS - 1).astype(jnp.int32)


def draw_near_count(key, part):
    counts = jax.random.randint(key, (CLUSTERS,), 1, KMAX + 1)
    owner = lax.broadcasted_iota(jnp.int32, (CLUSTERS,), 0) // NB_DEV
    boost = jnp.where(owner % 4 == 0, KMAX // 2, 0)
    counts = jnp.clip(counts + boost, 1, KMAX)
    return counts.at[0].set(KMAX).at[1].set(1).astype(jnp.int32)


def draw_cluster_rows(key, part):
    rows = jax.random.randint(key, (CLUSTERS,), BS // 2, BS + 1)
    return rows.at[0].set(BS).at[1].set(BS // 2).astype(jnp.int32)


def draw_far_list(key, part):
    offsets = jax.random.randint(key, (CLUSTERS, FMAX), NB_DEV + 1, CLUSTERS - NB_DEV)
    base = lax.broadcasted_iota(jnp.int32, (CLUSTERS, FMAX), 0)
    return ((base + offsets) % CLUSTERS).astype(jnp.int32)


def steps_of(rng, dims, cuts, smallest, top_value):
    loudness = 1.0
    for position, parts in cuts:
        steps = jax.random.uniform(jax.random.fold_in(jax.random.fold_in(rng, 6), position), (parts,), jnp.float32, smallest / len(cuts), top_value / len(cuts))
        loudness = loudness * jnp.repeat(jnp.exp(steps), dims[position] // parts).reshape((-1,) + (1,) * (len(dims) - 1 - position))
    return loudness


def gaussian(key, dims, width, reach, cuts=(), held_as=jnp.bfloat16):
    drawn = width * jax.random.normal(key, dims, jnp.float32)
    if cuts:
        drawn = drawn * steps_of(key, dims, cuts, -0.22, 0.18)
    return jnp.clip(drawn, -reach, reach).astype(held_as)


def setup_inputs(seed: int = 0, part: int = 0) -> dict:
    key_list = jax.random.split(jax.random.key(seed), 11)
    part_keys = jax.random.split(jax.random.fold_in(key_list[10], part), 11)
    probes = draw_probes(jax.random.fold_in(key_list[10], 71), part)
    near_blocks = draw_near_blocks(jax.random.fold_in(jax.random.fold_in(key_list[10], part), 71), part)
    near_list = draw_near_list(jax.random.fold_in(key_list[10], 71), part)
    near_count = draw_near_count(jax.random.fold_in(key_list[10], 71), part)
    cluster_rows = draw_cluster_rows(jax.random.fold_in(key_list[10], 71), part)
    row_basis = gaussian(part_keys[5], (CLUSTERS, 2, RANK, BS), RANK ** -0.5, 1.0, ((0, 32),))
    col_basis = gaussian(part_keys[6], (CLUSTERS, 2, RANK, BS), BS ** -0.5, 0.5, ((0, 32),))
    far_list = draw_far_list(jax.random.fold_in(key_list[10], 71), part)
    far_coupling = gaussian(part_keys[8], (CLUSTERS, FMAX, 2, RANK, RANK), (RANK * FMAX // 4) ** -0.5, 0.375, ((0, 32),), jnp.float32)
    weight = gaussian(part_keys[9], (2,), 2.0, 6.0, (), jnp.float32)
    return dict(probes=probes, near_blocks=near_blocks, near_list=near_list, near_count=near_count, cluster_rows=cluster_rows, row_basis=row_basis, col_basis=col_basis, far_list=far_list, far_coupling=far_coupling, weight=weight)


def operate(field, row_mask, near_blocks, near_list, slot_live, row_basis, col_basis, far_list, far_coupling):
    narrow = field.astype(jnp.bfloat16)
    pulled = narrow[near_list]
    pulled = jnp.where(slot_live[:, :, None, None, None], pulled, jnp.zeros((), jnp.bfloat16)).astype(jnp.float32)
    blocks = near_blocks.astype(jnp.float32)

    def prod(mat, vec):
        return jnp.einsum('nkrs,nkps->npr', mat, vec)
    near_re = prod(blocks[:, :, 0], pulled[:, :, 0]) - prod(blocks[:, :, 1], pulled[:, :, 1])
    near_im = prod(blocks[:, :, 0], pulled[:, :, 1]) + prod(blocks[:, :, 1], pulled[:, :, 0])
    basis = col_basis.astype(jnp.float32)
    wide = narrow.astype(jnp.float32)

    def contract(mat, vec):
        return jnp.einsum('nqr,npr->nqp', mat, vec)
    coef_re = contract(basis[:, 0], wide[:, 0]) - contract(basis[:, 1], wide[:, 1])
    coef_im = contract(basis[:, 0], wide[:, 1]) + contract(basis[:, 1], wide[:, 0])
    taken_re = coef_re[far_list]
    taken_im = coef_im[far_list]

    def couple(mat, vec):
        return jnp.einsum('nfqs,nfsp->nqp', mat, vec, precision=lax.Precision.HIGHEST)
    far_re = couple(far_coupling[:, :, 0], taken_re) - couple(far_coupling[:, :, 1], taken_im)
    far_im = couple(far_coupling[:, :, 0], taken_im) + couple(far_coupling[:, :, 1], taken_re)
    far_re = far_re.astype(jnp.bfloat16).astype(jnp.float32)
    far_im = far_im.astype(jnp.bfloat16).astype(jnp.float32)
    rows = row_basis.astype(jnp.float32)

    def expand(mat, vec):
        return jnp.einsum('nqr,nqp->npr', mat, vec)
    out_re = expand(rows[:, 0], far_re) - expand(rows[:, 1], far_im)
    out_im = expand(rows[:, 0], far_im) + expand(rows[:, 1], far_re)
    total = jnp.stack([near_re + out_re, near_im + out_im], axis=1)
    return total * row_mask

def inner(left, right):
    real_part = lax.optimization_barrier(jnp.sum(left[:, 0] * right[:, 0] + left[:, 1] * right[:, 1], axis=(0, 2)))
    imag_part = lax.optimization_barrier(jnp.sum(left[:, 0] * right[:, 1] - left[:, 1] * right[:, 0], axis=(0, 2)))
    return (real_part, imag_part)

def scaled(field, real_part, imag_part):
    sr = real_part[None, :, None]
    si = imag_part[None, :, None]
    return jnp.stack([sr * field[:, 0] - si * field[:, 1], sr * field[:, 1] + si * field[:, 0]], axis=1)

def reference(probes, near_blocks, near_list, near_count, cluster_rows, row_basis, col_basis, far_list, far_coupling, weight):
    rows_iota = lax.broadcasted_iota(jnp.int32, (probes.shape[0], probes.shape[3]), 1)
    row_mask = (rows_iota < cluster_rows[:, None]).astype(jnp.float32)[:, None, None, :]
    slots_iota = lax.broadcasted_iota(jnp.int32, near_list.shape, 1)
    slot_live = slots_iota < near_count[:, None]
    base = probes * row_mask

    def apply(field):
        return operate(field, row_mask, near_blocks, near_list, slot_live, row_basis, col_basis, far_list, far_coupling)
    beta = jnp.sqrt(lax.optimization_barrier(jnp.sum(base * base, axis=(0, 1, 3))) + 1e-06)
    first = base / beta[None, None, :, None]
    image_one = apply(first)
    proj_re, proj_im = inner(first, image_one)
    remain = image_one - scaled(first, proj_re, proj_im)
    size_two = jnp.sqrt(lax.optimization_barrier(jnp.sum(remain * remain, axis=(0, 1, 3))) + 1e-06)
    second = remain / size_two[None, None, :, None]
    factor = 1.0 / (CLUSTERS * BS)
    arnoldi = jnp.stack([beta * jnp.sqrt(jnp.float32(factor)), proj_re, proj_im, size_two], axis=0)
    image_two = apply(second)
    g11, zero_one = inner(image_one, image_one)
    g22, zero_two = inner(image_two, image_two)
    g12r, g12i = inner(image_one, image_two)
    q1r, q1i = inner(image_one, base)
    q2r, q2i = inner(image_two, base)
    det = g11 * g22 - (g12r * g12r + g12i * g12i)
    y1r = (g22 * q1r - (g12r * q2r - g12i * q2i)) / det
    y1i = (g22 * q1i - (g12r * q2i + g12i * q2r)) / det
    y2r = (g11 * q2r - (g12r * q1r + g12i * q1i)) / det
    y2i = (g11 * q2i - (g12r * q1i - g12i * q1r)) / det
    iterate = scaled(first, y1r, y1i) + scaled(second, y2r, y2i)
    wr = weight[0]
    wi = weight[1]
    solution = jnp.stack([wr * iterate[:, 0] - wi * iterate[:, 1], wr * iterate[:, 1] + wi * iterate[:, 0]], axis=1)
    mom_re = jnp.einsum('npr,nqr->pq', base[:, 0], iterate[:, 0], precision=lax.Precision.HIGHEST) + jnp.einsum('npr,nqr->pq', base[:, 1], iterate[:, 1], precision=lax.Precision.HIGHEST)
    mom_im = jnp.einsum('npr,nqr->pq', base[:, 0], iterate[:, 1], precision=lax.Precision.HIGHEST) - jnp.einsum('npr,nqr->pq', base[:, 1], iterate[:, 0], precision=lax.Precision.HIGHEST)
    moment = jnp.stack([wr * mom_re - wi * mom_im, wr * mom_im + wi * mom_re], axis=0) * factor
    return (solution, moment, arnoldi)
```

```python
import functools

import jax
import jax.numpy as jnp
from jax import lax
from jax.experimental import pallas as pl
from jax.experimental.pallas import tpu as pltpu
from jax.sharding import PartitionSpec as P


F32 = jnp.float32
BF16 = jnp.bfloat16
OWN = 8
RANK = 32
PROBES = 16
FMAX = 32
KMAX = 27
FAR_AT = 32
COUNT_AT = 64
ROWS_AT = 65
STAT = 64
PAY = 80
VMEM = pl.BlockSpec(memory_space=pltpu.VMEM)
SMEM = pl.BlockSpec(memory_space=pltpu.SMEM)


def dot_nt(left, right):
    return lax.dot_general(left, right, (((1,), (1,)), ((), ())), preferred_element_type=F32)


def dot_nn(left, right):
    return lax.dot_general(left, right, (((1,), (0,)), ((), ())), preferred_element_type=F32)


def dot_tn(left, right):
    return lax.dot_general(left, right, (((0,), (0,)), ((), ())), preferred_element_type=F32)


def lanes(rows):
    return lax.broadcasted_iota(jnp.int32, (rows, 128), 1)


def paired(field):
    re, im = field[:PROBES], field[PROBES:]
    return jnp.concatenate(
        [jnp.concatenate([re, -im], axis=1), jnp.concatenate([im, re], axis=1)], axis=0
    )


def high_low(value):
    high = value.astype(BF16)
    return high, (value - high.astype(F32)).astype(BF16)


def coefficients(pair, basis):
    both = jnp.concatenate([basis[0], basis[1]], axis=1)
    wide = dot_nt(both, jnp.concatenate([pair] * 4, axis=0))
    return wide


def pick_blocks(wide):
    block = lanes(8) // RANK
    out = jnp.where(block == 0, wide[0:8], 0.0)
    for b in range(1, 4):
        out = out + jnp.where(block == b, wide[8 * b : 8 * b + 8], 0.0)
    return out


def three_way(column, at):
    lane = lanes(PROBES)
    value = jnp.broadcast_to(column, (PROBES, 128))
    high = value.astype(BF16).astype(F32)
    rest = value - high
    mid = rest.astype(BF16).astype(F32)
    low = rest - mid
    zero = jnp.zeros((PROBES, 128), F32)
    return jnp.where(
        lane == at, high, jnp.where(lane == 32 + at, mid, jnp.where(lane == 64 + at, low, zero))
    )


def column_of(tile, *at):
    lane = lanes(PROBES)
    keep = lane == at[0]
    for a in at[1:]:
        keep = keep | (lane == a)
    return jnp.sum(jnp.where(keep, tile, 0.0), axis=1, keepdims=True)


def gathered_stat(mine, other):
    total = jnp.zeros((PROBES, 128), F32)
    for ref in (mine, other):
        for slot in range(16):
            total = total + ref[slot, STAT:PAY].astype(F32)
    return total


def lane_sum(value):
    return jnp.sum(value, axis=1, keepdims=True)


def twice(column):
    return jnp.concatenate([column, column], axis=0)


def front_kernel(meta, probes, col_basis, base, pay):
    lane = lanes(2 * PROBES)
    acc = jnp.zeros((PROBES, 128), F32)
    tiles = []
    for i in range(OWN):
        raw = jnp.concatenate([probes[i, 0], probes[i, 1]], axis=0)
        field = jnp.where(lane < meta[i, ROWS_AT], raw, 0.0)
        base[i] = field
        square = field * field
        acc = acc + square[:PROBES] + square[PROBES:]
        high, low = high_low(paired(field))
        basis = col_basis[i]
        tiles.append(pick_blocks(coefficients(high, basis) + coefficients(low, basis)))
    pay[0:STAT] = jnp.concatenate(tiles, axis=0).astype(BF16)
    pay[STAT:PAY] = three_way(lane_sum(acc), 0).astype(BF16)


def pack_kernel(coupling, packed):
    for g in range(FMAX // 4):
        four = [coupling[0, 4 * g + f].reshape(2 * RANK, RANK) for f in range(4)]
        high, low = high_low(jnp.concatenate(four, axis=1))
        packed[0, :, 128 * g : 128 * g + 128] = jnp.concatenate([high, low], axis=0)


def near_kernel(split, meta, own, partner, other, blocks, near, table):
    step = pl.program_id(0)

    @pl.when(step == 0)
    def _():
        for group, ref in enumerate((own, partner, other)):
            for i in range(OWN):
                field = ref[i].astype(F32)
                if split:
                    high, low = high_low(paired(field))
                    table[OWN * group + i] = jnp.concatenate([high, low], axis=0)
                else:
                    table[OWN * group + i] = paired(field).astype(BF16)

    height = table.shape[1]
    count = meta[step, COUNT_AT]

    def body(g, acc):
        for t in range(3):
            k = 3 * g + t
            vec = table[meta[step, k]]
            vec = jnp.where(k < count, vec, jnp.zeros_like(vec))
            mat = jnp.concatenate([blocks[0, k, 0], blocks[0, k, 1]], axis=1)
            acc = acc + dot_nt(vec, mat)
        return acc

    acc = lax.fori_loop(0, (count + 2) // 3, body, jnp.zeros((height, 128), F32))
    near[step] = acc[:32] + acc[32:] if split else acc


def far_part(i, meta, table, packed, row_basis):
    block = lanes(8) // RANK
    acc = jnp.zeros((128, 128), F32)
    for g in range(FMAX // 8):
        rows = []
        for f in range(8):
            tile = table[meta[i, FAR_AT + 8 * g + f]]
            for b in range(4):
                rows.append(jnp.where(block == b, tile, 0.0))
        taken = jnp.concatenate(rows, axis=0).astype(BF16)
        acc = acc + dot_nn(packed[i, :, 256 * g : 256 * g + 256], taken)
    both = acc[:64] + acc[64:]
    both = both + pltpu.roll(both, 64, 1)
    both = both + pltpu.roll(both, 32, 1)
    lane = lanes(RANK)
    sign = jnp.where((lane // PROBES) % 2 == 0, -1.0, 1.0)
    farcoef = both[:RANK] + sign * pltpu.roll(both[RANK:], PROBES, 1)
    turned = sign * pltpu.roll(farcoef, PROBES, 1)
    value = jnp.concatenate([farcoef, turned], axis=0)
    high, low = high_low(value)
    chosen = jnp.where(lanes(2 * RANK) < 32, high.astype(F32), low.astype(F32)).astype(BF16)
    basis = row_basis[i].reshape(2 * RANK, 128)
    out = dot_tn(chosen, basis)
    return out[0:32] + out[32:64]


def fill_table(mine, other, table):
    for half, ref in enumerate((mine, other)):
        for slot in range(16):
            at = 8 * (16 * half + slot)
            table[at : at + 8] = ref[slot, 0:STAT].astype(F32).reshape(8, 8, 128)


def image_kernel(
    meta, mine, other, packed, row_basis, col_basis, near, base, image, narrow, pay, keep, table, tiles
):
    fill_table(mine, other, table)
    beta = jnp.sqrt(column_of(gathered_stat(mine, other), 0, 32, 64) + 1e-06)
    inverse = twice(1.0 / beta)
    lane = lanes(2 * PROBES)

    def body(i, carry):
        acc_re, acc_im = carry
        far = far_part(i, meta, table, packed, row_basis)
        value = jnp.where(lane < meta[i, ROWS_AT], near[i] + far, 0.0) * inverse
        image[i] = value
        first = base[i] * inverse
        vr, vi = first[:PROBES], first[PROBES:]
        wr, wi = value[:PROBES], value[PROBES:]
        narrow[i] = value.astype(BF16)
        tiles[i] = pick_blocks(coefficients(paired(value).astype(BF16), col_basis[i]))
        return acc_re + vr * wr + vi * wi, acc_im + vr * wi - vi * wr

    zero = jnp.zeros((PROBES, 128), F32)
    acc_re, acc_im = lax.fori_loop(0, OWN, body, (zero, zero))
    pay[0:STAT] = tiles[...].reshape(STAT, 128).astype(BF16)
    pay[STAT:PAY] = (three_way(lane_sum(acc_re), 0) + three_way(lane_sum(acc_im), 1)).astype(BF16)
    keep[...] = jnp.broadcast_to(beta, (PROBES, 128))


def inner_kernel(
    meta, mine, other, packed, row_basis, near, base, image, keep, sums, head, table
):
    fill_table(mine, other, table)
    stat = gathered_stat(mine, other)
    hr = column_of(stat, 0, 32, 64)
    hi = column_of(stat, 1, 33, 65)
    beta = column_of(keep[...], 0)
    inverse = twice(1.0 / beta)
    lane = lanes(2 * PROBES)
    high = lax.Precision.HIGHEST

    def times_h(field):
        re, im = field[:PROBES], field[PROBES:]
        return jnp.concatenate([hr * re - hi * im, hr * im + hi * re], axis=0)

    def body(i, carry):
        acc, mom = carry
        far = far_part(i, meta, table, packed, row_basis)
        second = jnp.where(lane < meta[i, ROWS_AT], near[i] + far, 0.0)
        w = image[i]
        b = base[i]
        v = b * inverse
        t = w - times_h(v)
        u = second - times_h(w)
        wr, wi, ur, ui = w[:PROBES], w[PROBES:], u[:PROBES], u[PROBES:]
        br, bi, tr, ti = b[:PROBES], b[PROBES:], t[:PROBES], t[PROBES:]
        vr, vi = v[:PROBES], v[PROBES:]
        terms = (
            tr * tr + ti * ti,
            wr * ur + wi * ui,
            wr * ui - wi * ur,
            ur * ur + ui * ui,
            ur * br + ui * bi,
            ur * bi - ui * br,
            wr * wr + wi * wi,
            wr * br + wi * bi,
            wr * bi - wi * br,
        )
        acc = tuple(a + x for a, x in zip(acc, terms))
        left = jnp.concatenate(
            [jnp.concatenate([vr, vi], axis=1), jnp.concatenate([tr, ti], axis=1)], axis=0
        )
        one = jnp.concatenate([br, bi], axis=1)
        two = jnp.concatenate([-bi, br], axis=1)
        zero = jnp.zeros_like(one)
        right = jnp.concatenate([zero, one, two, one, two, zero, zero, zero], axis=0)
        mom = mom + lax.dot_general(
            left, right, (((1,), (1,)), ((), ())), precision=high, preferred_element_type=F32
        )
        return acc, mom

    zero = jnp.zeros((PROBES, 128), F32)
    acc, mom = lax.fori_loop(
        0, OWN, body, (tuple(zero for _ in range(9)), jnp.zeros((2 * PROBES, 128), F32))
    )
    short = lanes(PROBES)
    tile = jnp.where(short < 48, mom[:PROBES], mom[PROBES:])
    tile = jnp.where((short >= 16) & (short < 80), tile, 0.0)
    for k, term in enumerate(acc):
        tile = tile + jnp.where(short == k, lane_sum(term), 0.0)
    sums[...] = tile
    head[...] = jnp.where(short == 0, beta, jnp.where(short == 1, hr, jnp.where(short == 2, hi, 0.0)))


def final_kernel(weight, sums, head, base, image, solution, moment, arnoldi):
    tile = sums[...]
    top = head[...]
    beta, hr, hi = (column_of(top, k) for k in range(3))
    t2, g12r, g12i, g22, q2r, q2i, g11, q1r, q1i = (column_of(tile, k) for k in range(9))
    size = jnp.sqrt(t2 + 1e-06)
    inv = 1.0 / size
    g12r, g12i, q2r, q2i = g12r * inv, g12i * inv, q2r * inv, q2i * inv
    g22 = g22 * inv * inv
    det = g11 * g22 - (g12r * g12r + g12i * g12i)
    y1r = (g22 * q1r - (g12r * q2r - g12i * q2i)) / det
    y1i = (g22 * q1i - (g12r * q2i + g12i * q2r)) / det
    y2r = (g11 * q2r - (g12r * q1r + g12i * q1i)) / det * inv
    y2i = (g11 * q2i - (g12r * q1i - g12i * q1r)) / det * inv
    wr, wi = weight[0], weight[1]
    factor = 1.0 / (256 * 128)
    inverse = 1.0 / beta
    for i in range(OWN):
        vr, vi = base[i, :PROBES] * inverse, base[i, PROBES:] * inverse
        tr = image[i, :PROBES] - (hr * vr - hi * vi)
        ti = image[i, PROBES:] - (hr * vi + hi * vr)
        xr = (y1r * vr - y1i * vi) + (y2r * tr - y2i * ti)
        xi = (y1r * vi + y1i * vr) + (y2r * ti + y2i * tr)
        solution[i, 0] = wr * xr - wi * xi
        solution[i, 1] = wr * xi + wi * xr
    lane = lanes(PROBES)
    sign = jnp.where(lane < 32, -1.0, 1.0)

    def turned(x):
        return sign * jnp.where(lane < 32, pltpu.roll(x, 112, 1), pltpu.roll(x, 16, 1))

    late = pltpu.roll(tile, 96, 1)
    mom = (y1r * tile + y1i * turned(tile)) + (y2r * late + y2i * turned(late))
    mom = (wr * mom + wi * turned(mom)) * factor
    root = jnp.sqrt(jnp.full((1, 1), factor, F32))
    out = jnp.where((lane >= 16) & (lane < 48), mom, 0.0)
    for k, column in enumerate((beta * root, hr, hi, size)):
        out = jnp.where(lane == k, column, out)
    turned_out = jnp.transpose(out)
    moment[0] = turned_out[16:32]
    moment[1] = turned_out[32:48]
    arnoldi[...] = turned_out[0:4]


def shape(dims, dtype=F32):
    return jax.ShapeDtypeStruct(dims, dtype)


def params(mib):
    return pltpu.CompilerParams(vmem_limit_bytes=mib << 20)


def z_step(d):
    return [(i, (i & ~6) | ((((i >> 1) + d) & 3) << 1)) for i in range(32)]


def y_step(d):
    return [(i, (i & 7) | ((((i >> 3) + d) & 3) << 3)) for i in range(32)]


CORE = [(i, i ^ 1) for i in range(32)]
SIDE = [(i, i + 1 if i % 2 else i - 1) for i in range(1, 31)]


def send(x, pairs):
    return lax.ppermute(x, "clus", pairs)


def gather_all(pay):
    four = jnp.stack([pay] + [send(pay, z_step(d)) for d in (1, 2, 3)], axis=0)
    mine = jnp.concatenate([four] + [send(four, y_step(d)) for d in (1, 2, 3)], axis=0)
    return mine, send(mine, CORE)


def add_all(x):
    for step in (z_step, y_step):
        x = x + send(x, step(1)) + send(x, step(2)) + send(x, step(3))
    return x + send(x, CORE)


def shards(
    probes,
    near_blocks,
    near_list,
    near_count,
    cluster_rows,
    row_basis,
    col_basis,
    far_list,
    far_coupling,
    weight,
):
    me = lax.axis_index("clus")
    first = me * OWN
    local = near_list - first
    flip = (me % 2) * OWN
    near_at = jnp.where(
        local < 0, local + 2 * OWN + OWN - flip, jnp.where(local < OWN, local, local + flip)
    )
    owner = far_list // OWN
    hop_z = ((me // 2) - (owner // 2)) % 4
    hop_y = ((me // 8) - (owner // 8)) % 4
    slot = (((me ^ owner) & 1) * 4 + hop_y) * 4 + hop_z
    far_at = slot * OWN + far_list % OWN
    meta = jnp.concatenate(
        [
            near_at,
            jnp.zeros((OWN, FAR_AT - KMAX), jnp.int32),
            far_at,
            near_count[:, None],
            cluster_rows[:, None],
            jnp.zeros((OWN, 62), jnp.int32),
        ],
        axis=1,
    ).astype(jnp.int32)

    base, pay = pl.pallas_call(
        front_kernel,
        out_shape=(shape((OWN, 32, 128)), shape((PAY, 128), BF16)),
        in_specs=[SMEM, VMEM, VMEM],
        out_specs=(VMEM, VMEM),
        compiler_params=params(4),
        name="front",
    )(meta, probes, col_basis)

    packed = pl.pallas_call(
        pack_kernel,
        grid=(OWN,),
        out_shape=shape((OWN, 128, 1024), BF16),
        in_specs=[pl.BlockSpec((1, FMAX, 2, RANK, RANK), lambda i: (i, 0, 0, 0, 0))],
        out_specs=pl.BlockSpec((1, 128, 1024), lambda i: (i, 0, 0)),
        compiler_params=params(8),
        name="pack",
    )(far_coupling)

    def near_product(split, own, partner, other):
        whole = pl.BlockSpec((OWN, 32, 128), lambda i: (0, 0, 0))
        return pl.pallas_call(
            functools.partial(near_kernel, split),
            grid=(OWN,),
            out_shape=shape((OWN, 32, 128)),
            in_specs=[SMEM, whole, whole, whole]
            + [pl.BlockSpec((1, KMAX, 2, 128, 128), lambda i: (i, 0, 0, 0, 0))],
            out_specs=whole,
            scratch_shapes=[pltpu.VMEM((3 * OWN, 64 if split else 32, 256), BF16)],
            compiler_params=params(10),
            cost_estimate=pl.CostEstimate(
                flops=8 * 27 * 4 * 2 * 128 * 128 * 16, bytes_accessed=14 << 20, transcendentals=0
            ),
            name="near",
        )(meta, own, partner, other, near_blocks)

    near_one = near_product(True, base, send(base, CORE), send(base, SIDE))
    mine, other = gather_all(pay)
    image, narrow, pay_two, keep = pl.pallas_call(
        image_kernel,
        out_shape=(
            shape((OWN, 32, 128)),
            shape((OWN, 32, 128), BF16),
            shape((PAY, 128), BF16),
            shape((PROBES, 128)),
        ),
        in_specs=[SMEM] + [VMEM] * 7,
        out_specs=(VMEM,) * 4,
        scratch_shapes=[pltpu.VMEM((256, 8, 128), F32), pltpu.VMEM((OWN, 8, 128), F32)],
        compiler_params=params(10),
        name="image",
    )(meta, mine, other, packed, row_basis, col_basis, near_one, base)

    near_two = near_product(False, narrow, send(narrow, CORE), send(narrow, SIDE))
    mine, other = gather_all(pay_two)
    sums, head = pl.pallas_call(
        inner_kernel,
        out_shape=(shape((PROBES, 128)), shape((PROBES, 128))),
        in_specs=[SMEM] + [VMEM] * 8,
        out_specs=(VMEM, VMEM),
        scratch_shapes=[pltpu.VMEM((256, 8, 128), F32)],
        compiler_params=params(10),
        name="inner",
    )(meta, mine, other, packed, row_basis, near_two, base, image, keep)

    return pl.pallas_call(
        final_kernel,
        out_shape=(shape((OWN, 2, PROBES, 128)), shape((2, PROBES, PROBES)), shape((4, PROBES))),
        in_specs=[SMEM] + [VMEM] * 4,
        out_specs=(VMEM,) * 3,
        compiler_params=params(4),
        name="final",
    )(weight, add_all(sums), head, base, image)


def solution(mesh):
    in_specs = (
        P("clus", None, None, None),
        P(("contour", "clus"), None, None, None, None),
        P("clus", None),
        P("clus"),
        P("clus"),
        P(("contour", "clus"), None, None, None),
        P(("contour", "clus"), None, None, None),
        P("clus", None),
        P(("contour", "clus"), None, None, None, None),
        P("contour"),
    )
    out_specs = (
        P(("contour", "clus"), None, None, None),
        P("contour", None, None),
        P("contour", None),
    )
    return jax.shard_map(shards, mesh=mesh, in_specs=in_specs, out_specs=out_specs, check_vma=False)
```

```python
import functools

import jax
import jax.numpy as jnp
from jax import lax
from jax.experimental import pallas as pl
from jax.experimental.pallas import tpu as pltpu
from jax.sharding import PartitionSpec as P


F32 = jnp.float32
BF16 = jnp.bfloat16
OWN = 8
RANK = 32
PROBES = 16
FMAX = 32
KMAX = 27
NEAR_SPLIT = (3, 3, 2)
STAT = 64
PAY = 80
VMEM = pl.BlockSpec(memory_space=pltpu.VMEM)
SMEM = pl.BlockSpec(memory_space=pltpu.SMEM)


def dot_nt(left, right):
    return lax.dot_general(left, right, (((1,), (1,)), ((), ())), preferred_element_type=F32)


def dot_nn(left, right):
    return lax.dot_general(left, right, (((1,), (0,)), ((), ())), preferred_element_type=F32)


def dot_tn(left, right):
    return lax.dot_general(left, right, (((0,), (0,)), ((), ())), preferred_element_type=F32)


def lanes(rows):
    return lax.broadcasted_iota(jnp.int32, (rows, 128), 1)


def paired(field):
    re, im = field[:PROBES], field[PROBES:]
    return jnp.concatenate(
        [jnp.concatenate([re, -im], axis=1), jnp.concatenate([im, re], axis=1)], axis=0
    )


def high_low(value):
    high = value.astype(BF16)
    return high, (value - high.astype(F32)).astype(BF16)


def coefficients(pair, basis):
    both = jnp.concatenate([basis[0], basis[1]], axis=1)
    return dot_nt(both, jnp.concatenate([pair] * 4, axis=0))


def side_by_side(wide):
    block = lanes(RANK) // RANK
    return jnp.where(
        block < 2,
        jnp.where(block == 0, wide[0], wide[1]),
        jnp.where(block == 2, wide[2], wide[3]),
    )


def three_way(column, at):
    lane = lanes(PROBES)
    value = jnp.broadcast_to(column, (PROBES, 128))
    high = value.astype(BF16).astype(F32)
    rest = value - high
    mid = rest.astype(BF16).astype(F32)
    low = rest - mid
    zero = jnp.zeros((PROBES, 128), F32)
    return jnp.where(
        lane == at, high, jnp.where(lane == 32 + at, mid, jnp.where(lane == 64 + at, low, zero))
    )


def column_of(tile, *at):
    lane = lanes(PROBES)
    keep = lane == at[0]
    for a in at[1:]:
        keep = keep | (lane == a)
    return jnp.sum(jnp.where(keep, tile, 0.0), axis=1, keepdims=True)


def gathered_stat(mine, other):
    total = jnp.zeros((PROBES, 128), F32)
    for ref in (mine, other):
        for slot in range(16):
            total = total + ref[slot, STAT:PAY].astype(F32)
    return total


def lane_sum(value):
    return jnp.sum(value, axis=1, keepdims=True)


def twice(column):
    return jnp.concatenate([column, column], axis=0)


def front_kernel(rows, near_list, far_list, probes, col_basis, base, pay, near_at, far_at):
    me = lax.axis_index("clus")
    local = near_list[...] - me * OWN
    flip = (me & 1) * OWN
    near_at[...] = jnp.where(
        local < 0, local + 3 * OWN - flip, jnp.where(local < OWN, local, local + flip)
    )
    far = far_list[...]
    owner = far >> 3
    hop_z = ((me >> 1) - (owner >> 1)) & 3
    hop_y = ((me >> 3) - (owner >> 3)) & 3
    place_z = jnp.where(hop_z > 1, 5 - hop_z, hop_z)
    place_y = jnp.where(hop_y > 1, 5 - hop_y, hop_y)
    slot = (((me ^ owner) & 1) * 4 + place_y) * 4 + place_z
    far_at[...] = slot * OWN + (far & 7)

    lane = lanes(2 * PROBES)
    acc = jnp.zeros((PROBES, 128), F32)
    fields = []
    for i in range(OWN):
        raw = jnp.concatenate([probes[i, 0], probes[i, 1]], axis=0)
        field = jnp.where(lane < rows[i], raw, 0.0)
        base[i] = field
        fields.append(field)
        square = field * field
        acc = acc + square[:PROBES] + square[PROBES:]
    wide = []
    for i in range(OWN):
        high, low = high_low(paired(fields[i]))
        basis = col_basis[i]
        wide.append(coefficients(high, basis) + coefficients(low, basis))
    pay[0:32] = side_by_side(wide[:4]).astype(BF16)
    pay[32:64] = side_by_side(wide[4:]).astype(BF16)
    pay[STAT:PAY] = three_way(lane_sum(acc), 0).astype(BF16)


def pack_kernel(first, coupling, packed):
    for i in range(packed.shape[0]):
        for g in range(FMAX // 4):
            four = [coupling[first + i, 4 * g + f].reshape(2 * RANK, RANK) for f in range(4)]
            high, low = high_low(jnp.concatenate(four, axis=1))
            packed[i, :, 128 * g : 128 * g + 128] = jnp.concatenate([high, low], axis=0)


def near_kernel(first, split, fill, near_at, near_count, *refs):
    if fill:
        own, partner, other, blocks, near, table = refs
        for group, ref in enumerate((own, partner, other)):
            for i in range(OWN):
                field = ref[i].astype(F32)
                if split:
                    high, low = high_low(paired(field))
                    table[OWN * group + i] = jnp.concatenate([high, low], axis=0)
                else:
                    table[OWN * group + i] = paired(field).astype(BF16)
    else:
        table, blocks, near = refs
    count = near.shape[0]
    acc = [jnp.zeros((128, table.shape[1]), F32) for _ in range(count)]
    for k in range(KMAX):
        for i in range(count):
            vec = table[near_at[first + i, k]]
            vec = jnp.where(k < near_count[first + i], vec, jnp.zeros_like(vec))
            mat = jnp.concatenate([blocks[first + i, k, 0], blocks[first + i, k, 1]], axis=1)
            acc[i] = acc[i] + dot_nt(mat, vec)
    for i in range(count):
        out = jnp.transpose(acc[i])
        near[i] = out[:32] + out[32:] if split else out


def far_fields(far_at, mine, other, packs, row_basis, table, masks):
    for half, ref in enumerate((mine, other)):
        for slot in range(16):
            at = 2 * (16 * half + slot)
            table[at : at + 2] = ref[slot, 0:STAT].reshape(2, RANK, 128)
    block = lanes(RANK) // RANK
    for b in range(4):
        masks[b] = jnp.where(block == b, 1.0, 0.0).astype(BF16)
    folded = []
    for i in range(OWN):
        rows = []
        for f in range(FMAX):
            at = far_at[i, f]
            rows.append(table[at >> 2] * masks[at & 3])
        packed = packs[i // (OWN // 2)]
        acc = dot_nn(packed[i % (OWN // 2)], jnp.concatenate(rows, axis=0))
        folded.append(acc[:64] + acc[64:])
    both = jnp.concatenate(folded, axis=0)
    both = both + pltpu.roll(both, 64, 1)
    both = both + pltpu.roll(both, 32, 1)
    both = both.reshape(OWN, 2, RANK, 128)
    real, imag = (both[:, c].reshape(OWN * RANK, 128) for c in range(2))
    lane = lanes(OWN * RANK)
    sign = jnp.where((lane // PROBES) % 2 == 0, -1.0, 1.0)
    farcoef = real + sign * pltpu.roll(imag, PROBES, 1)
    turned = sign * pltpu.roll(farcoef, PROBES, 1)
    chosen = []
    for value in (farcoef, turned):
        high = value.astype(BF16).astype(F32)
        chosen.append(jnp.where(lane < 32, high, value - high).astype(BF16))
    out = []
    for i in range(OWN):
        span = slice(RANK * i, RANK * i + RANK)
        left = jnp.concatenate([chosen[0][span], chosen[1][span]], axis=0)
        out.append(dot_tn(left, row_basis[i].reshape(2 * RANK, 128)))
    return [x[0:32] + x[32:64] for x in out]


def image_kernel(far_at, rows, mine, other, *refs):
    pack_a, pack_b, row_basis, col_basis, *nears, base, image, narrow, pay, keep, table, masks = refs
    far = far_fields(far_at, mine, other, (pack_a, pack_b), row_basis, table, masks)
    beta = jnp.sqrt(column_of(gathered_stat(mine, other), 0, 32, 64) + 1e-06)
    inverse = twice(1.0 / beta)
    lane = lanes(2 * PROBES)
    near = [ref[i] for ref in nears for i in range(ref.shape[0])]
    acc_re = jnp.zeros((PROBES, 128), F32)
    acc_im = jnp.zeros((PROBES, 128), F32)
    values = []
    for i in range(OWN):
        value = jnp.where(lane < rows[i], near[i] + far[i], 0.0) * inverse
        values.append(value)
        image[i] = value
        narrow[i] = value.astype(BF16)
    wide = [coefficients(paired(values[i]).astype(BF16), col_basis[i]) for i in range(OWN)]
    for i in range(OWN):
        first = base[i] * inverse
        vr, vi = first[:PROBES], first[PROBES:]
        wr, wi = values[i][:PROBES], values[i][PROBES:]
        acc_re = acc_re + vr * wr + vi * wi
        acc_im = acc_im + vr * wi - vi * wr
    pay[0:32] = side_by_side(wide[:4]).astype(BF16)
    pay[32:64] = side_by_side(wide[4:]).astype(BF16)
    pay[STAT:PAY] = (three_way(lane_sum(acc_re), 0) + three_way(lane_sum(acc_im), 1)).astype(BF16)
    keep[...] = jnp.broadcast_to(beta, (PROBES, 128))


def inner_kernel(far_at, rows, mine, other, *refs):
    pack_a, pack_b, row_basis, *nears, base, image, keep, sums, head, table, masks = refs
    far = far_fields(far_at, mine, other, (pack_a, pack_b), row_basis, table, masks)
    stat = gathered_stat(mine, other)
    hr = column_of(stat, 0, 32, 64)
    hi = column_of(stat, 1, 33, 65)
    beta = column_of(keep[...], 0)
    inverse = twice(1.0 / beta)
    lane = lanes(2 * PROBES)
    near = [ref[i] for ref in nears for i in range(ref.shape[0])]

    def times_h(field):
        re, im = field[:PROBES], field[PROBES:]
        return jnp.concatenate([hr * re - hi * im, hr * im + hi * re], axis=0)

    acc = [jnp.zeros((PROBES, 128), F32) for _ in range(9)]
    left, right = [], []
    for i in range(OWN):
        second = jnp.where(lane < rows[i], near[i] + far[i], 0.0)
        w = image[i]
        b = base[i]
        v = b * inverse
        t = w - times_h(v)
        u = second - times_h(w)
        wr, wi, ur, ui = w[:PROBES], w[PROBES:], u[:PROBES], u[PROBES:]
        br, bi, tr, ti = b[:PROBES], b[PROBES:], t[:PROBES], t[PROBES:]
        vr, vi = v[:PROBES], v[PROBES:]
        terms = (
            tr * tr + ti * ti,
            wr * ur + wi * ui,
            wr * ui - wi * ur,
            ur * ur + ui * ui,
            ur * br + ui * bi,
            ur * bi - ui * br,
            wr * wr + wi * wi,
            wr * br + wi * bi,
            wr * bi - wi * br,
        )
        acc = [a + x for a, x in zip(acc, terms)]
        left.append(
            jnp.concatenate(
                [jnp.concatenate([vr, vi], axis=1), jnp.concatenate([tr, ti], axis=1)], axis=0
            )
        )
        right.append(
            jnp.concatenate(
                [jnp.concatenate([br, bi], axis=1), jnp.concatenate([-bi, br], axis=1)], axis=0
            )
        )
    mom = lax.dot_general(
        jnp.concatenate(left, axis=1),
        jnp.concatenate(right, axis=1),
        (((1,), (1,)), ((), ())),
        precision=lax.Precision.HIGHEST,
        preferred_element_type=F32,
    )
    short = lanes(PROBES)
    wide = jnp.concatenate([mom, jnp.zeros((2 * PROBES, 96), F32)], axis=1)
    tile = jnp.where(
        (short >= 16) & (short < 48), pltpu.roll(wide[:PROBES], 16, 1), 0.0
    ) + jnp.where((short >= 48) & (short < 80), pltpu.roll(wide[PROBES:], 48, 1), 0.0)
    for k, term in enumerate(acc):
        tile = tile + jnp.where(short == k, lane_sum(term), 0.0)
    sums[...] = tile
    head[...] = jnp.where(short == 0, beta, jnp.where(short == 1, hr, jnp.where(short == 2, hi, 0.0)))


def final_kernel(weight, sums, head, base, image, solution, moment, arnoldi):
    tile = sums[0]
    for slot in range(1, sums.shape[0]):
        tile = tile + sums[slot]
    top = head[...]
    beta, hr, hi = (column_of(top, k) for k in range(3))
    t2, g12r, g12i, g22, q2r, q2i, g11, q1r, q1i = (column_of(tile, k) for k in range(9))
    size = jnp.sqrt(t2 + 1e-06)
    inv = 1.0 / size
    g12r, g12i, q2r, q2i = g12r * inv, g12i * inv, q2r * inv, q2i * inv
    g22 = g22 * inv * inv
    det = g11 * g22 - (g12r * g12r + g12i * g12i)
    y1r = (g22 * q1r - (g12r * q2r - g12i * q2i)) / det
    y1i = (g22 * q1i - (g12r * q2i + g12i * q2r)) / det
    y2r = (g11 * q2r - (g12r * q1r + g12i * q1i)) / det * inv
    y2i = (g11 * q2i - (g12r * q1i - g12i * q1r)) / det * inv
    wr, wi = weight[0], weight[1]
    factor = 1.0 / (256 * 128)
    inverse = 1.0 / beta
    for i in range(OWN):
        vr, vi = base[i, :PROBES] * inverse, base[i, PROBES:] * inverse
        tr = image[i, :PROBES] - (hr * vr - hi * vi)
        ti = image[i, PROBES:] - (hr * vi + hi * vr)
        xr = (y1r * vr - y1i * vi) + (y2r * tr - y2i * ti)
        xi = (y1r * vi + y1i * vr) + (y2r * ti + y2i * tr)
        solution[i, 0] = wr * xr - wi * xi
        solution[i, 1] = wr * xi + wi * xr
    lane = lanes(PROBES)
    sign = jnp.where(lane < 32, -1.0, 1.0)

    def turned(x):
        return sign * jnp.where(lane < 32, pltpu.roll(x, 112, 1), pltpu.roll(x, 16, 1))

    late = pltpu.roll(tile, 96, 1)
    mom = (y1r * tile + y1i * turned(tile)) + (y2r * late + y2i * turned(late))
    mom = (wr * mom + wi * turned(mom)) * factor
    root = jnp.sqrt(jnp.full((1, 1), factor, F32))
    out = jnp.where((lane >= 16) & (lane < 48), mom, 0.0)
    for k, column in enumerate((beta * root, hr, hi, size)):
        out = jnp.where(lane == k, column, out)
    turned_out = jnp.transpose(out)
    moment[0] = turned_out[16:32]
    moment[1] = turned_out[32:48]
    arnoldi[...] = turned_out[0:4]


def shape(dims, dtype=F32):
    return jax.ShapeDtypeStruct(dims, dtype)


def params(mib):
    return pltpu.CompilerParams(vmem_limit_bytes=mib << 20)


def z_step(d):
    return [(i, (i & ~6) | ((((i >> 1) + d) & 3) << 1)) for i in range(32)]


def y_step(d):
    return [(i, (i & 7) | ((((i >> 3) + d) & 3) << 3)) for i in range(32)]


CORE = [(i, i ^ 1) for i in range(32)]
SIDE = [(i, i + 1 if i % 2 else i - 1) for i in range(1, 31)]


def send(x, pairs):
    return lax.ppermute(x, "clus", pairs)


def gather_ring(x, step):
    low = send(x, step(1))
    high = send(x, step(3))
    last = send(low, step(1))
    return jnp.concatenate([x, low, high, last], axis=0)


def gather_all(pay):
    four = gather_ring(pay[None], z_step)
    mine = gather_ring(four, y_step)
    return mine, send(mine, CORE)


def shards(
    probes,
    near_blocks,
    near_list,
    near_count,
    cluster_rows,
    row_basis,
    col_basis,
    far_list,
    far_coupling,
    weight,
):
    base, pay, near_at, far_at = pl.pallas_call(
        front_kernel,
        out_shape=(
            shape((OWN, 32, 128)),
            shape((PAY, 128), BF16),
            shape((OWN, KMAX), jnp.int32),
            shape((OWN, FMAX), jnp.int32),
        ),
        in_specs=[SMEM] + [VMEM] * 4,
        out_specs=(VMEM,) * 4,
        compiler_params=params(4),
        name="front",
    )(cluster_rows, near_list, far_list, probes, col_basis)

    def pack(first):
        half = OWN // 2
        return pl.pallas_call(
            functools.partial(pack_kernel, first),
            out_shape=shape((half, 128, 1024), BF16),
            in_specs=[VMEM],
            out_specs=VMEM,
            compiler_params=params(10),
            cost_estimate=pl.CostEstimate(flops=1 << 20, bytes_accessed=5 << 20, transcendentals=0),
            name="pack",
        )(far_coupling)

    def near_products(split, field):
        partner = send(field, CORE)
        other = send(field, SIDE)
        height = 64 if split else 32
        nears, table, at = [], None, 0
        for part, size in enumerate(NEAR_SPLIT):
            fill = part == 0
            out = pl.pallas_call(
                functools.partial(near_kernel, at, split, fill),
                out_shape=(shape((size, 32, 128)),)
                + ((shape((3 * OWN, height, 256), BF16),) if fill else ()),
                in_specs=[SMEM, SMEM] + [VMEM] * (4 if fill else 2),
                out_specs=(VMEM,) * (2 if fill else 1),
                compiler_params=params(16),
                cost_estimate=pl.CostEstimate(
                    flops=size * KMAX * 8 * 128 * 128 * 16,
                    bytes_accessed=size * KMAX << 16,
                    transcendentals=0,
                ),
                name="near",
            )(near_at, near_count, *((field, partner, other) if fill else (table,)), near_blocks)
            if fill:
                table = out[1]
            nears.append(out[0])
            at += size
        return nears

    packs = (pack(0), pack(OWN // 2))
    nears = near_products(True, base)
    mine, other = gather_all(pay)
    scratch = [pltpu.VMEM((64, RANK, 128), BF16), pltpu.VMEM((4, RANK, 128), BF16)]
    image, narrow, pay_two, keep = pl.pallas_call(
        image_kernel,
        out_shape=(
            shape((OWN, 32, 128)),
            shape((OWN, 32, 128), BF16),
            shape((PAY, 128), BF16),
            shape((PROBES, 128)),
        ),
        in_specs=[SMEM, SMEM] + [VMEM] * (7 + len(nears)),
        out_specs=(VMEM,) * 4,
        scratch_shapes=scratch,
        compiler_params=params(10),
        name="image",
    )(far_at, cluster_rows, mine, other, *packs, row_basis, col_basis, *nears, base)

    nears = near_products(False, narrow)
    mine, other = gather_all(pay_two)
    sums, head = pl.pallas_call(
        inner_kernel,
        out_shape=(shape((PROBES, 128)), shape((PROBES, 128))),
        in_specs=[SMEM, SMEM] + [VMEM] * (8 + len(nears)),
        out_specs=(VMEM, VMEM),
        scratch_shapes=scratch,
        compiler_params=params(10),
        name="inner",
    )(far_at, cluster_rows, mine, other, *packs, row_basis, *nears, base, image, keep)

    spread = jnp.broadcast_to(sums[None], (32, PROBES, 128))
    return pl.pallas_call(
        final_kernel,
        out_shape=(shape((OWN, 2, PROBES, 128)), shape((2, PROBES, PROBES)), shape((4, PROBES))),
        in_specs=[SMEM] + [VMEM] * 4,
        out_specs=(VMEM,) * 3,
        compiler_params=params(4),
        name="final",
    )(weight, lax.all_to_all(spread, "clus", 0, 0), head, base, image)


def solution(mesh):
    in_specs = (
        P("clus", None, None, None),
        P(("contour", "clus"), None, None, None, None),
        P("clus", None),
        P("clus"),
        P("clus"),
        P(("contour", "clus"), None, None, None),
        P(("contour", "clus"), None, None, None),
        P("clus", None),
        P(("contour", "clus"), None, None, None, None),
        P("contour"),
    )
    out_specs = (
        P(("contour", "clus"), None, None, None),
        P("contour", None, None),
        P("contour", None),
    )
    return jax.shard_map(shards, mesh=mesh, in_specs=in_specs, out_specs=out_specs, check_vma=False)
```

```python
import functools

import jax
import jax.numpy as jnp
from jax import lax
from jax.experimental import pallas as pl
from jax.experimental.pallas import tpu as pltpu
from jax.sharding import PartitionSpec as P


F32 = jnp.float32
BF16 = jnp.bfloat16
OWN = 8
RANK = 32
PROBES = 16
FMAX = 32
KMAX = 27
FRONT_MIB = 56
NEAR_MIB = 47
STAT = 64
PAY = 80
VMEM = pl.BlockSpec(memory_space=pltpu.VMEM)
SMEM = pl.BlockSpec(memory_space=pltpu.SMEM)
HBM = pl.BlockSpec(memory_space=pltpu.HBM)
ANY = pl.BlockSpec(memory_space=pl.ANY)


def dot_nt(left, right):
    return lax.dot_general(left, right, (((1,), (1,)), ((), ())), preferred_element_type=F32)


def dot_nn(left, right):
    return lax.dot_general(left, right, (((1,), (0,)), ((), ())), preferred_element_type=F32)


def dot_tn(left, right):
    return lax.dot_general(left, right, (((0,), (0,)), ((), ())), preferred_element_type=F32)


def lanes(rows):
    return lax.broadcasted_iota(jnp.int32, (rows, 128), 1)


def paired(field):
    re, im = field[:PROBES], field[PROBES:]
    return jnp.concatenate(
        [jnp.concatenate([re, -im], axis=1), jnp.concatenate([im, re], axis=1)], axis=0
    )


def high_low(value):
    high = value.astype(BF16)
    return high, (value - high.astype(F32)).astype(BF16)


def coefficients(pair, basis):
    both = jnp.concatenate([basis[0], basis[1]], axis=1)
    return dot_nt(both, jnp.concatenate([pair] * 4, axis=0))


def side_by_side(wide):
    block = lanes(RANK) // RANK
    return jnp.where(
        block < 2,
        jnp.where(block == 0, wide[0], wide[1]),
        jnp.where(block == 2, wide[2], wide[3]),
    )


def three_way(column, at):
    lane = lanes(PROBES)
    value = jnp.broadcast_to(column, (PROBES, 128))
    high = value.astype(BF16).astype(F32)
    rest = value - high
    mid = rest.astype(BF16).astype(F32)
    low = rest - mid
    zero = jnp.zeros((PROBES, 128), F32)
    return jnp.where(
        lane == at, high, jnp.where(lane == 32 + at, mid, jnp.where(lane == 64 + at, low, zero))
    )


def column_of(tile, *at):
    lane = lanes(PROBES)
    keep = lane == at[0]
    for a in at[1:]:
        keep = keep | (lane == a)
    return jnp.sum(jnp.where(keep, tile, 0.0), axis=1, keepdims=True)


def gathered_stat(mine, other):
    total = jnp.zeros((PROBES, 128), F32)
    for ref in (mine, other):
        for slot in range(16):
            total = total + ref[slot, STAT:PAY].astype(F32)
    return total


def lane_sum(value):
    return jnp.sum(value, axis=1, keepdims=True)


def twice(column):
    return jnp.concatenate([column, column], axis=0)


def spread_out(pay, spread, sems):
    copies = [
        pltpu.make_async_copy(pay, spread.at[n], sems.at[n]) for n in range(spread.shape[0])
    ]
    for copy in copies:
        copy.start()
    for copy in copies:
        copy.wait()


def front_kernel(*refs):
    sources, (base, spread), held, (pay, sems, out_sems) = refs[:3], refs[3:5], refs[5:8], refs[8:]
    copies = [
        pltpu.make_async_copy(src, dst, sems.at[n])
        for n, (src, dst) in enumerate(zip(sources, held))
    ]
    for copy in copies:
        copy.start()
    rows, probes, col_basis = held
    for copy in copies:
        copy.wait()
    lane = lanes(2 * PROBES)
    acc = jnp.zeros((PROBES, 128), F32)
    fields = []
    for i in range(OWN):
        raw = jnp.concatenate([probes[i, 0], probes[i, 1]], axis=0)
        field = jnp.where(lane < rows[i], raw, 0.0)
        base[i] = field
        fields.append(field)
        square = field * field
        acc = acc + square[:PROBES] + square[PROBES:]
    wide = []
    for i in range(OWN):
        high, low = high_low(paired(fields[i]))
        basis = col_basis[i]
        wide.append(coefficients(high, basis) + coefficients(low, basis))
    pay[0:32] = side_by_side(wide[:4]).astype(BF16)
    pay[32:64] = side_by_side(wide[4:]).astype(BF16)
    pay[STAT:PAY] = three_way(lane_sum(acc), 0).astype(BF16)
    spread_out(pay, spread, out_sems)


def pack_one(coupling, packed, i):
    for g in range(FMAX // 4):
        four = [coupling[i, 4 * g + f].reshape(2 * RANK, RANK) for f in range(4)]
        high, low = high_low(jnp.concatenate(four, axis=1))
        packed[i, :, 128 * g : 128 * g + 128] = jnp.concatenate([high, low], axis=0)


def near_kernel(split, near_list, near_count, *refs):
    if split:
        far_list, source, partner, other, blocks, coupling = refs[:6]
        near, packed, far_at, table, held, sems, kept, more, own, own_sem = refs[6:]
        fetch = pltpu.make_async_copy(source, own, own_sem)
        fetch.start()
    else:
        own, partner, other, blocks, near, table, held, sems = refs
    piece = KMAX // 3

    def copy(i, j):
        span = pl.ds(piece * j, piece)
        return pltpu.make_async_copy(blocks.at[i, span], held.at[i, span], sems.at[i, j])

    def copy_more(i):
        return pltpu.make_async_copy(coupling.at[i], kept.at[i], more.at[i])

    for i in range(OWN):
        for j in range(3):
            copy(i, j).start()
    if split:
        for i in range(OWN):
            copy_more(i).start()
    me = lax.axis_index("clus")
    flip = (me & 1) * OWN
    if split:
        far = far_list[...]
        owner = far >> 3
        far_at[...] = (((me ^ owner) & 1) * 16 + (owner >> 1)) * OWN + (far & 7)
        fetch.wait()

    def place(i, k):
        local = near_list[i, k] - me * OWN
        return jnp.where(
            local < 0, local + 3 * OWN - flip, jnp.where(local < OWN, local, local + flip)
        )

    for group, ref in enumerate((own, partner, other)):
        for i in range(OWN):
            field = ref[i].astype(F32)
            if split:
                high, low = high_low(paired(field))
                table[OWN * group + i] = jnp.concatenate([high, low], axis=0)
            else:
                table[OWN * group + i] = paired(field).astype(BF16)
    for i in range(OWN):
        acc = jnp.zeros((128, table.shape[1]), F32)
        for j in range(3):
            copy(i, j).wait()
            for k in range(piece * j, piece * j + piece):
                vec = table[place(i, k)]
                vec = jnp.where(k < near_count[i], vec, jnp.zeros_like(vec))
                mat = jnp.concatenate([held[i, k, 0], held[i, k, 1]], axis=1)
                acc = acc + dot_nt(mat, vec)
        out = jnp.transpose(acc)
        near[i] = out[:32] + out[32:] if split else out
    if split:
        for i in range(OWN):
            copy_more(i).wait()
            pack_one(kept, packed, i)


def far_fields(far_at, mine, other, packed, row_basis, table, masks):
    for half, ref in enumerate((mine, other)):
        for slot in range(16):
            at = 2 * (16 * half + slot)
            table[at : at + 2] = ref[slot, 0:STAT].reshape(2, RANK, 128)
    block = lanes(RANK) // RANK
    for b in range(4):
        masks[b] = jnp.where(block == b, 1.0, 0.0).astype(BF16)
    folded = []
    for i in range(OWN):
        rows = []
        for f in range(FMAX):
            at = far_at[i, f]
            rows.append(table[at >> 2] * masks[at & 3])
        acc = dot_nn(packed[i], jnp.concatenate(rows, axis=0))
        folded.append(acc[:64] + acc[64:])
    both = jnp.concatenate(folded, axis=0)
    both = both + pltpu.roll(both, 64, 1)
    both = both + pltpu.roll(both, 32, 1)
    both = both.reshape(OWN, 2, RANK, 128)
    real, imag = (both[:, c].reshape(OWN * RANK, 128) for c in range(2))
    lane = lanes(OWN * RANK)
    sign = jnp.where((lane // PROBES) % 2 == 0, -1.0, 1.0)
    farcoef = real + sign * pltpu.roll(imag, PROBES, 1)
    turned = sign * pltpu.roll(farcoef, PROBES, 1)
    chosen = []
    for value in (farcoef, turned):
        high = value.astype(BF16).astype(F32)
        chosen.append(jnp.where(lane < 32, high, value - high).astype(BF16))
    out = []
    for i in range(OWN):
        span = slice(RANK * i, RANK * i + RANK)
        left = jnp.concatenate([chosen[0][span], chosen[1][span]], axis=0)
        out.append(dot_tn(left, row_basis[i].reshape(2 * RANK, 128)))
    return [x[0:32] + x[32:64] for x in out]


def image_kernel(far_at, rows, mine, other, *refs):
    packed, row_basis, col_basis, near, base, image, narrow, spread, keep = refs[:9]
    table, masks, pay, out_sems = refs[9:]
    far = far_fields(far_at, mine, other, packed, row_basis, table, masks)
    beta = jnp.sqrt(column_of(gathered_stat(mine, other), 0, 32, 64) + 1e-06)
    inverse = twice(1.0 / beta)
    lane = lanes(2 * PROBES)
    acc_re = jnp.zeros((PROBES, 128), F32)
    acc_im = jnp.zeros((PROBES, 128), F32)
    values = []
    for i in range(OWN):
        value = jnp.where(lane < rows[i], near[i] + far[i], 0.0) * inverse
        values.append(value)
        image[i] = value
        narrow[i] = value.astype(BF16)
    wide = [coefficients(paired(values[i]).astype(BF16), col_basis[i]) for i in range(OWN)]
    for i in range(OWN):
        first = base[i] * inverse
        vr, vi = first[:PROBES], first[PROBES:]
        wr, wi = values[i][:PROBES], values[i][PROBES:]
        acc_re = acc_re + vr * wr + vi * wi
        acc_im = acc_im + vr * wi - vi * wr
    pay[0:32] = side_by_side(wide[:4]).astype(BF16)
    pay[32:64] = side_by_side(wide[4:]).astype(BF16)
    pay[STAT:PAY] = (three_way(lane_sum(acc_re), 0) + three_way(lane_sum(acc_im), 1)).astype(BF16)
    keep[...] = jnp.broadcast_to(beta, (PROBES, 128))
    spread_out(pay, spread, out_sems)


def inner_kernel(far_at, rows, mine, other, *refs):
    packed, row_basis, near, base, image, keep, sums, head, table, masks = refs
    far = far_fields(far_at, mine, other, packed, row_basis, table, masks)
    stat = gathered_stat(mine, other)
    hr = column_of(stat, 0, 32, 64)
    hi = column_of(stat, 1, 33, 65)
    beta = column_of(keep[...], 0)
    inverse = twice(1.0 / beta)
    lane = lanes(2 * PROBES)

    def times_h(field):
        re, im = field[:PROBES], field[PROBES:]
        return jnp.concatenate([hr * re - hi * im, hr * im + hi * re], axis=0)

    acc = [jnp.zeros((PROBES, 128), F32) for _ in range(9)]
    left, right = [], []
    for i in range(OWN):
        second = jnp.where(lane < rows[i], near[i] + far[i], 0.0)
        w = image[i]
        b = base[i]
        v = b * inverse
        t = w - times_h(v)
        u = second - times_h(w)
        wr, wi, ur, ui = w[:PROBES], w[PROBES:], u[:PROBES], u[PROBES:]
        br, bi, tr, ti = b[:PROBES], b[PROBES:], t[:PROBES], t[PROBES:]
        vr, vi = v[:PROBES], v[PROBES:]
        terms = (
            tr * tr + ti * ti,
            wr * ur + wi * ui,
            wr * ui - wi * ur,
            ur * ur + ui * ui,
            ur * br + ui * bi,
            ur * bi - ui * br,
            wr * wr + wi * wi,
            wr * br + wi * bi,
            wr * bi - wi * br,
        )
        acc = [a + x for a, x in zip(acc, terms)]
        left.append(
            jnp.concatenate(
                [jnp.concatenate([vr, vi], axis=1), jnp.concatenate([tr, ti], axis=1)], axis=0
            )
        )
        right.append(
            jnp.concatenate(
                [jnp.concatenate([br, bi], axis=1), jnp.concatenate([-bi, br], axis=1)], axis=0
            )
        )
    mom = lax.dot_general(
        jnp.concatenate(left, axis=1),
        jnp.concatenate(right, axis=1),
        (((1,), (1,)), ((), ())),
        precision=lax.Precision.HIGHEST,
        preferred_element_type=F32,
    )
    short = lanes(PROBES)
    wide = jnp.concatenate([mom, jnp.zeros((2 * PROBES, 96), F32)], axis=1)
    tile = jnp.where(
        (short >= 16) & (short < 48), pltpu.roll(wide[:PROBES], 16, 1), 0.0
    ) + jnp.where((short >= 48) & (short < 80), pltpu.roll(wide[PROBES:], 48, 1), 0.0)
    for k, term in enumerate(acc):
        tile = tile + jnp.where(short == k, lane_sum(term), 0.0)
    sums[...] = tile
    head[...] = jnp.where(short == 0, beta, jnp.where(short == 1, hr, jnp.where(short == 2, hi, 0.0)))


def final_kernel(weight, sums, head, base, image, solution, moment, arnoldi):
    tile = sums[0]
    for slot in range(1, sums.shape[0]):
        tile = tile + sums[slot]
    top = head[...]
    beta, hr, hi = (column_of(top, k) for k in range(3))
    t2, g12r, g12i, g22, q2r, q2i, g11, q1r, q1i = (column_of(tile, k) for k in range(9))
    size = jnp.sqrt(t2 + 1e-06)
    inv = 1.0 / size
    g12r, g12i, q2r, q2i = g12r * inv, g12i * inv, q2r * inv, q2i * inv
    g22 = g22 * inv * inv
    det = g11 * g22 - (g12r * g12r + g12i * g12i)
    y1r = (g22 * q1r - (g12r * q2r - g12i * q2i)) / det
    y1i = (g22 * q1i - (g12r * q2i + g12i * q2r)) / det
    y2r = (g11 * q2r - (g12r * q1r + g12i * q1i)) / det * inv
    y2i = (g11 * q2i - (g12r * q1i - g12i * q1r)) / det * inv
    wr, wi = weight[0], weight[1]
    factor = 1.0 / (256 * 128)
    inverse = 1.0 / beta
    for i in range(OWN):
        vr, vi = base[i, :PROBES] * inverse, base[i, PROBES:] * inverse
        tr = image[i, :PROBES] - (hr * vr - hi * vi)
        ti = image[i, PROBES:] - (hr * vi + hi * vr)
        xr = (y1r * vr - y1i * vi) + (y2r * tr - y2i * ti)
        xi = (y1r * vi + y1i * vr) + (y2r * ti + y2i * tr)
        solution[i, 0] = wr * xr - wi * xi
        solution[i, 1] = wr * xi + wi * xr
    lane = lanes(PROBES)
    sign = jnp.where(lane < 32, -1.0, 1.0)

    def turned(x):
        return sign * jnp.where(lane < 32, pltpu.roll(x, 112, 1), pltpu.roll(x, 16, 1))

    late = pltpu.roll(tile, 96, 1)
    mom = (y1r * tile + y1i * turned(tile)) + (y2r * late + y2i * turned(late))
    mom = (wr * mom + wi * turned(mom)) * factor
    root = jnp.sqrt(jnp.full((1, 1), factor, F32))
    out = jnp.where((lane >= 16) & (lane < 48), mom, 0.0)
    for k, column in enumerate((beta * root, hr, hi, size)):
        out = jnp.where(lane == k, column, out)
    turned_out = jnp.transpose(out)
    moment[0] = turned_out[16:32]
    moment[1] = turned_out[32:48]
    arnoldi[...] = turned_out[0:4]


def shape(dims, dtype=F32):
    return jax.ShapeDtypeStruct(dims, dtype)


def params(mib):
    return pltpu.CompilerParams(vmem_limit_bytes=mib << 20)


CORE = [(i, i ^ 1) for i in range(32)]
SIDE = [(i, (i + 1 if i % 2 else i - 1) % 32) for i in range(32)]
COLUMNS = [list(range(k, 32, 2)) for k in range(2)]


def send(x, pairs):
    return lax.ppermute(x, "clus", pairs)


def gather_all(copies):
    mine = lax.all_to_all(copies, "clus", 0, 0, axis_index_groups=COLUMNS)
    return mine, send(mine, CORE)


def shards(
    probes,
    near_blocks,
    near_list,
    near_count,
    cluster_rows,
    row_basis,
    col_basis,
    far_list,
    far_coupling,
    weight,
):
    base, spread = pl.pallas_call(
        front_kernel,
        out_shape=(shape((OWN, 32, 128)), shape((16, PAY, 128), BF16)),
        in_specs=[HBM] * 3,
        out_specs=(VMEM, ANY),
        scratch_shapes=[
            pltpu.SMEM((OWN,), jnp.int32),
            pltpu.VMEM((OWN, 2, PROBES, 128), F32),
            pltpu.VMEM((OWN, 2, RANK, 128), BF16),
            pltpu.VMEM((PAY, 128), BF16),
            pltpu.SemaphoreType.DMA((3,)),
            pltpu.SemaphoreType.DMA((16,)),
        ],
        compiler_params=params(FRONT_MIB),
        name="front",
    )(cluster_rows, probes, col_basis)

    def near_product(split, field):
        partner = send(field, CORE)
        other = send(field, SIDE)
        blocks_shape = (OWN, KMAX, 2, 128, 128)
        coupling_shape = (OWN, FMAX, 2, RANK, RANK)
        out_shape = (shape((OWN, 32, 128)),)
        scratch = [
            pltpu.VMEM((3 * OWN, 64 if split else 32, 256), BF16),
            pltpu.VMEM(blocks_shape, BF16),
            pltpu.SemaphoreType.DMA((OWN, 3)),
        ]
        arguments = (near_list, near_count, field, partner, other, near_blocks)
        in_specs = [SMEM, SMEM, VMEM, VMEM, VMEM, HBM]
        if split:
            out_shape += (shape((OWN, 128, 1024), BF16), shape((OWN, FMAX), jnp.int32))
            scratch += [
                pltpu.VMEM(coupling_shape, F32),
                pltpu.SemaphoreType.DMA((OWN,)),
                pltpu.VMEM((OWN, 32, 128), F32),
                pltpu.SemaphoreType.DMA,
            ]
            arguments = arguments[:2] + (far_list,) + arguments[2:] + (far_coupling,)
            in_specs = [SMEM, SMEM, VMEM, ANY, VMEM, VMEM, HBM, HBM]
        return pl.pallas_call(
            functools.partial(near_kernel, split),
            out_shape=out_shape,
            in_specs=in_specs,
            out_specs=(VMEM,) * len(out_shape),
            scratch_shapes=scratch,
            compiler_params=params(NEAR_MIB),
            cost_estimate=pl.CostEstimate(
                flops=OWN * KMAX * 8 * 128 * 128 * 16,
                bytes_accessed=OWN * KMAX << 16,
                transcendentals=0,
            ),
            name="near",
        )(*arguments)

    near, packed, far_at = near_product(True, base)
    mine, other = gather_all(spread)
    scratch = [pltpu.VMEM((64, RANK, 128), BF16), pltpu.VMEM((4, RANK, 128), BF16)]
    image, narrow, spread, keep = pl.pallas_call(
        image_kernel,
        out_shape=(
            shape((OWN, 32, 128)),
            shape((OWN, 32, 128), BF16),
            shape((16, PAY, 128), BF16),
            shape((PROBES, 128)),
        ),
        in_specs=[SMEM, SMEM] + [VMEM] * 7,
        out_specs=(VMEM, VMEM, ANY, VMEM),
        scratch_shapes=scratch + [pltpu.VMEM((PAY, 128), BF16), pltpu.SemaphoreType.DMA((16,))],
        compiler_params=params(10),
        name="image",
    )(far_at, cluster_rows, mine, other, packed, row_basis, col_basis, near, base)

    (near,) = near_product(False, narrow)
    mine, other = gather_all(spread)
    sums, head = pl.pallas_call(
        inner_kernel,
        out_shape=(shape((PROBES, 128)), shape((PROBES, 128))),
        in_specs=[SMEM, SMEM] + [VMEM] * 8,
        out_specs=(VMEM, VMEM),
        scratch_shapes=scratch,
        compiler_params=params(10),
        name="inner",
    )(far_at, cluster_rows, mine, other, packed, row_basis, near, base, image, keep)

    spread = jnp.broadcast_to(sums[None], (32, PROBES, 128))
    return pl.pallas_call(
        final_kernel,
        out_shape=(shape((OWN, 2, PROBES, 128)), shape((2, PROBES, PROBES)), shape((4, PROBES))),
        in_specs=[SMEM] + [VMEM] * 4,
        out_specs=(VMEM,) * 3,
        compiler_params=params(4),
        name="final",
    )(weight, lax.all_to_all(spread, "clus", 0, 0), head, base, image)


def solution(mesh):
    in_specs = (
        P("clus", None, None, None),
        P(("contour", "clus"), None, None, None, None),
        P("clus", None),
        P("clus"),
        P("clus"),
        P(("contour", "clus"), None, None, None),
        P(("contour", "clus"), None, None, None),
        P("clus", None),
        P(("contour", "clus"), None, None, None, None),
        P("contour"),
    )
    out_specs = (
        P(("contour", "clus"), None, None, None),
        P("contour", None, None),
        P("contour", None),
    )
    return jax.shard_map(shards, mesh=mesh, in_specs=in_specs, out_specs=out_specs, check_vma=False)
```

```python
import functools

import jax
import jax.numpy as jnp
from jax import lax
from jax.experimental import pallas as pl
from jax.experimental.pallas import tpu as pltpu
from jax.sharding import PartitionSpec as P


F32 = jnp.float32
BF16 = jnp.bfloat16
OWN = 8
RANK = 32
PROBES = 16
FMAX = 32
KMAX = 27
FRONT_MIB = 2
PIECES = ((0, 1), (1, 2), (3, 2), (5, 3))
PACK_PIECES = ((0, 4), (4, 2), (6, 2))
NEAR_MIB = 47
STAT = 64
PAY = 80
VMEM = pl.BlockSpec(memory_space=pltpu.VMEM)
SMEM = pl.BlockSpec(memory_space=pltpu.SMEM)
HBM = pl.BlockSpec(memory_space=pltpu.HBM)
ANY = pl.BlockSpec(memory_space=pl.ANY)


def dot_nt(left, right):
    return lax.dot_general(left, right, (((1,), (1,)), ((), ())), preferred_element_type=F32)


def dot_nn(left, right):
    return lax.dot_general(left, right, (((1,), (0,)), ((), ())), preferred_element_type=F32)


def dot_tn(left, right):
    return lax.dot_general(left, right, (((0,), (0,)), ((), ())), preferred_element_type=F32)


def lanes(rows):
    return lax.broadcasted_iota(jnp.int32, (rows, 128), 1)


def paired(field):
    re, im = field[:PROBES], field[PROBES:]
    return jnp.concatenate(
        [jnp.concatenate([re, -im], axis=1), jnp.concatenate([im, re], axis=1)], axis=0
    )


def high_low(value):
    high = value.astype(BF16)
    return high, (value - high.astype(F32)).astype(BF16)


def coefficients(pair, basis):
    both = jnp.concatenate([basis[0], basis[1]], axis=1)
    return dot_nt(both, jnp.concatenate([pair] * 4, axis=0))


def side_by_side(wide):
    block = lanes(RANK) // RANK
    return jnp.where(
        block < 2,
        jnp.where(block == 0, wide[0], wide[1]),
        jnp.where(block == 2, wide[2], wide[3]),
    )


def three_way(column, at):
    lane = lanes(PROBES)
    value = jnp.broadcast_to(column, (PROBES, 128))
    high = value.astype(BF16).astype(F32)
    rest = value - high
    mid = rest.astype(BF16).astype(F32)
    low = rest - mid
    zero = jnp.zeros((PROBES, 128), F32)
    return jnp.where(
        lane == at, high, jnp.where(lane == 32 + at, mid, jnp.where(lane == 64 + at, low, zero))
    )


def column_of(tile, *at):
    lane = lanes(PROBES)
    keep = lane == at[0]
    for a in at[1:]:
        keep = keep | (lane == a)
    return jnp.sum(jnp.where(keep, tile, 0.0), axis=1, keepdims=True)


def gathered_stat(mine, other):
    total = jnp.zeros((PROBES, 128), F32)
    for ref in (mine, other):
        for slot in range(16):
            total = total + ref[slot, STAT:PAY].astype(F32)
    return total


def lane_sum(value):
    return jnp.sum(value, axis=1, keepdims=True)


def twice(column):
    return jnp.concatenate([column, column], axis=0)


def spread_out(pay, spread, sems):
    copies = [
        pltpu.make_async_copy(pay, spread.at[n], sems.at[n]) for n in range(spread.shape[0])
    ]
    for copy in copies:
        copy.start()
    for copy in copies:
        copy.wait()


def front_kernel(rows, probes, col_basis, base, spread, pay, out_sems):
    lane = lanes(2 * PROBES)
    acc = jnp.zeros((PROBES, 128), F32)
    fields = []
    for i in range(OWN):
        raw = jnp.concatenate([probes[i, 0], probes[i, 1]], axis=0)
        field = jnp.where(lane < rows[i], raw, 0.0)
        base[i] = field
        fields.append(field)
        square = field * field
        acc = acc + square[:PROBES] + square[PROBES:]
    wide = []
    for i in range(OWN):
        high, low = high_low(paired(fields[i]))
        basis = col_basis[i]
        wide.append(coefficients(high, basis) + coefficients(low, basis))
    pay[0:32] = side_by_side(wide[:4]).astype(BF16)
    pay[32:64] = side_by_side(wide[4:]).astype(BF16)
    pay[STAT:PAY] = three_way(lane_sum(acc), 0).astype(BF16)
    spread_out(pay, spread, out_sems)


def pack_one(coupling, packed, i):
    for g in range(FMAX // 4):
        four = [coupling[i, 4 * g + f].reshape(2 * RANK, RANK) for f in range(4)]
        high, low = high_low(jnp.concatenate(four, axis=1))
        packed[i, :, 128 * g : 128 * g + 128] = jnp.concatenate([high, low], axis=0)


def near_kernel(split, near_list, near_count, *refs):
    if split:
        far_list, own, partner, other, blocks, coupling, near, packed, far_at = refs[:9]
        table, held, sems, kept, more = refs[9:]
    else:
        own, partner, other, blocks, near, table, held, sems = refs
    pieces = [
        pltpu.make_async_copy(
            blocks.at[pl.ds(at, size)], held.at[pl.ds(at, size)], sems.at[n]
        )
        for n, (at, size) in enumerate(PIECES)
    ]
    for piece in pieces:
        piece.start()
    me = lax.axis_index("clus")
    flip = (me & 1) * OWN
    if split:
        late = [
            pltpu.make_async_copy(
                coupling.at[pl.ds(at, size)], kept.at[pl.ds(at, size)], more.at[n]
            )
            for n, (at, size) in enumerate(PACK_PIECES)
        ]
        for piece in late:
            piece.start()
        far = far_list[...]
        owner = far >> 3
        far_at[...] = (((me ^ owner) & 1) * 16 + (owner >> 1)) * OWN + (far & 7)

    def place(i, k):
        local = near_list[i, k] - me * OWN
        return jnp.where(
            local < 0, local + 3 * OWN - flip, jnp.where(local < OWN, local, local + flip)
        )

    for group, ref in enumerate((own, partner, other)):
        for i in range(OWN):
            field = ref[i].astype(F32)
            if split:
                high, low = high_low(paired(field))
                table[OWN * group + i] = jnp.concatenate([high, low], axis=0)
            else:
                table[OWN * group + i] = paired(field).astype(BF16)
    for (at, size), piece in zip(PIECES, pieces):
        piece.wait()
        acc = [jnp.zeros((128, table.shape[1]), F32) for _ in range(size)]
        for k in range(KMAX):
            for j in range(size):
                vec = table[place(at + j, k)]
                vec = jnp.where(k < near_count[at + j], vec, jnp.zeros_like(vec))
                mat = jnp.concatenate([held[at + j, k, 0], held[at + j, k, 1]], axis=1)
                acc[j] = acc[j] + dot_nt(mat, vec)
        for j in range(size):
            out = jnp.transpose(acc[j])
            near[at + j] = out[:32] + out[32:] if split else out
    if split:
        for (at, size), piece in zip(PACK_PIECES, late):
            piece.wait()
            for i in range(at, at + size):
                pack_one(kept, packed, i)


def far_fields(far_at, mine, other, packed, row_basis, table, masks):
    for half, ref in enumerate((mine, other)):
        for slot in range(16):
            at = 2 * (16 * half + slot)
            table[at : at + 2] = ref[slot, 0:STAT].reshape(2, RANK, 128)
    block = lanes(RANK) // RANK
    for b in range(4):
        masks[b] = jnp.where(block == b, 1.0, 0.0).astype(BF16)
    folded = []
    for i in range(OWN):
        rows = []
        for f in range(FMAX):
            at = far_at[i, f]
            rows.append(table[at >> 2] * masks[at & 3])
        acc = dot_nn(packed[i], jnp.concatenate(rows, axis=0))
        folded.append(acc[:64] + acc[64:])
    both = jnp.concatenate(folded, axis=0)
    both = both + pltpu.roll(both, 64, 1)
    both = both + pltpu.roll(both, 32, 1)
    both = both.reshape(OWN, 2, RANK, 128)
    real, imag = (both[:, c].reshape(OWN * RANK, 128) for c in range(2))
    lane = lanes(OWN * RANK)
    sign = jnp.where((lane // PROBES) % 2 == 0, -1.0, 1.0)
    farcoef = real + sign * pltpu.roll(imag, PROBES, 1)
    turned = sign * pltpu.roll(farcoef, PROBES, 1)
    chosen = []
    for value in (farcoef, turned):
        high = value.astype(BF16).astype(F32)
        chosen.append(jnp.where(lane < 32, high, value - high).astype(BF16))
    out = []
    for i in range(OWN):
        span = slice(RANK * i, RANK * i + RANK)
        left = jnp.concatenate([chosen[0][span], chosen[1][span]], axis=0)
        out.append(dot_tn(left, row_basis[i].reshape(2 * RANK, 128)))
    return [x[0:32] + x[32:64] for x in out]


def image_kernel(far_at, rows, mine, other, *refs):
    packed, row_basis, col_basis, near, base, image, narrow, spread, keep = refs[:-4]
    table, masks, pay, out_sems = refs[-4:]
    far = far_fields(far_at, mine, other, packed, row_basis, table, masks)
    beta = jnp.sqrt(column_of(gathered_stat(mine, other), 0, 32, 64) + 1e-06)
    inverse = twice(1.0 / beta)
    lane = lanes(2 * PROBES)
    acc_re = jnp.zeros((PROBES, 128), F32)
    acc_im = jnp.zeros((PROBES, 128), F32)
    values = []
    for i in range(OWN):
        value = jnp.where(lane < rows[i], near[i] + far[i], 0.0) * inverse
        values.append(value)
        image[i] = value
        narrow[i] = value.astype(BF16)
    wide = [coefficients(paired(values[i]).astype(BF16), col_basis[i]) for i in range(OWN)]
    for i in range(OWN):
        first = base[i] * inverse
        vr, vi = first[:PROBES], first[PROBES:]
        wr, wi = values[i][:PROBES], values[i][PROBES:]
        acc_re = acc_re + vr * wr + vi * wi
        acc_im = acc_im + vr * wi - vi * wr
    pay[0:32] = side_by_side(wide[:4]).astype(BF16)
    pay[32:64] = side_by_side(wide[4:]).astype(BF16)
    pay[STAT:PAY] = (three_way(lane_sum(acc_re), 0) + three_way(lane_sum(acc_im), 1)).astype(BF16)
    keep[...] = jnp.broadcast_to(beta, (PROBES, 128))
    spread_out(pay, spread, out_sems)


def inner_kernel(far_at, rows, mine, other, *refs):
    packed, row_basis, near, base, image, keep, sums, head, table, masks = refs
    far = far_fields(far_at, mine, other, packed, row_basis, table, masks)
    stat = gathered_stat(mine, other)
    hr = column_of(stat, 0, 32, 64)
    hi = column_of(stat, 1, 33, 65)
    beta = column_of(keep[...], 0)
    inverse = twice(1.0 / beta)
    lane = lanes(2 * PROBES)

    def times_h(field):
        re, im = field[:PROBES], field[PROBES:]
        return jnp.concatenate([hr * re - hi * im, hr * im + hi * re], axis=0)

    acc = [jnp.zeros((PROBES, 128), F32) for _ in range(9)]
    left, right = [], []
    for i in range(OWN):
        second = jnp.where(lane < rows[i], near[i] + far[i], 0.0)
        w = image[i]
        b = base[i]
        v = b * inverse
        t = w - times_h(v)
        u = second - times_h(w)
        wr, wi, ur, ui = w[:PROBES], w[PROBES:], u[:PROBES], u[PROBES:]
        br, bi, tr, ti = b[:PROBES], b[PROBES:], t[:PROBES], t[PROBES:]
        vr, vi = v[:PROBES], v[PROBES:]
        terms = (
            tr * tr + ti * ti,
            wr * ur + wi * ui,
            wr * ui - wi * ur,
            ur * ur + ui * ui,
            ur * br + ui * bi,
            ur * bi - ui * br,
            wr * wr + wi * wi,
            wr * br + wi * bi,
            wr * bi - wi * br,
        )
        acc = [a + x for a, x in zip(acc, terms)]
        left.append(
            jnp.concatenate(
                [jnp.concatenate([vr, vi], axis=1), jnp.concatenate([tr, ti], axis=1)], axis=0
            )
        )
        right.append(
            jnp.concatenate(
                [jnp.concatenate([br, bi], axis=1), jnp.concatenate([-bi, br], axis=1)], axis=0
            )
        )
    mom = lax.dot_general(
        jnp.concatenate(left, axis=1),
        jnp.concatenate(right, axis=1),
        (((1,), (1,)), ((), ())),
        precision=lax.Precision.HIGHEST,
        preferred_element_type=F32,
    )
    short = lanes(PROBES)
    wide = jnp.concatenate([mom, jnp.zeros((2 * PROBES, 96), F32)], axis=1)
    tile = jnp.where(
        (short >= 16) & (short < 48), pltpu.roll(wide[:PROBES], 16, 1), 0.0
    ) + jnp.where((short >= 48) & (short < 80), pltpu.roll(wide[PROBES:], 48, 1), 0.0)
    for k, term in enumerate(acc):
        tile = tile + jnp.where(short == k, lane_sum(term), 0.0)
    sums[...] = tile
    head[...] = jnp.where(short == 0, beta, jnp.where(short == 1, hr, jnp.where(short == 2, hi, 0.0)))


def final_kernel(weight, sums, head, base, image, solution, moment, arnoldi):
    tile = sums[0]
    for slot in range(1, sums.shape[0]):
        tile = tile + sums[slot]
    top = head[...]
    beta, hr, hi = (column_of(top, k) for k in range(3))
    t2, g12r, g12i, g22, q2r, q2i, g11, q1r, q1i = (column_of(tile, k) for k in range(9))
    size = jnp.sqrt(t2 + 1e-06)
    inv = 1.0 / size
    g12r, g12i, q2r, q2i = g12r * inv, g12i * inv, q2r * inv, q2i * inv
    g22 = g22 * inv * inv
    det = g11 * g22 - (g12r * g12r + g12i * g12i)
    y1r = (g22 * q1r - (g12r * q2r - g12i * q2i)) / det
    y1i = (g22 * q1i - (g12r * q2i + g12i * q2r)) / det
    y2r = (g11 * q2r - (g12r * q1r + g12i * q1i)) / det * inv
    y2i = (g11 * q2i - (g12r * q1i - g12i * q1r)) / det * inv
    wr, wi = weight[0], weight[1]
    factor = 1.0 / (256 * 128)
    inverse = 1.0 / beta
    for i in range(OWN):
        vr, vi = base[i, :PROBES] * inverse, base[i, PROBES:] * inverse
        tr = image[i, :PROBES] - (hr * vr - hi * vi)
        ti = image[i, PROBES:] - (hr * vi + hi * vr)
        xr = (y1r * vr - y1i * vi) + (y2r * tr - y2i * ti)
        xi = (y1r * vi + y1i * vr) + (y2r * ti + y2i * tr)
        solution[i, 0] = wr * xr - wi * xi
        solution[i, 1] = wr * xi + wi * xr
    lane = lanes(PROBES)
    sign = jnp.where(lane < 32, -1.0, 1.0)

    def turned(x):
        return sign * jnp.where(lane < 32, pltpu.roll(x, 112, 1), pltpu.roll(x, 16, 1))

    late = pltpu.roll(tile, 96, 1)
    mom = (y1r * tile + y1i * turned(tile)) + (y2r * late + y2i * turned(late))
    mom = (wr * mom + wi * turned(mom)) * factor
    root = jnp.sqrt(jnp.full((1, 1), factor, F32))
    out = jnp.where((lane >= 16) & (lane < 48), mom, 0.0)
    for k, column in enumerate((beta * root, hr, hi, size)):
        out = jnp.where(lane == k, column, out)
    turned_out = jnp.transpose(out)
    moment[0] = turned_out[16:32]
    moment[1] = turned_out[32:48]
    arnoldi[...] = turned_out[0:4]


def shape(dims, dtype=F32):
    return jax.ShapeDtypeStruct(dims, dtype)


def params(mib):
    return pltpu.CompilerParams(vmem_limit_bytes=mib << 20)


CORE = [(i, i ^ 1) for i in range(32)]
SIDE = [(i, (i + 1 if i % 2 else i - 1) % 32) for i in range(32)]
COLUMNS = [list(range(k, 32, 2)) for k in range(2)]


def send(x, pairs):
    return lax.ppermute(x, "clus", pairs)


def gather_all(copies):
    mine = lax.all_to_all(copies, "clus", 0, 0, axis_index_groups=COLUMNS)
    return mine, send(mine, CORE)


def shards(
    probes,
    near_blocks,
    near_list,
    near_count,
    cluster_rows,
    row_basis,
    col_basis,
    far_list,
    far_coupling,
    weight,
):
    base, spread = pl.pallas_call(
        front_kernel,
        out_shape=(shape((OWN, 32, 128)), shape((16, PAY, 128), BF16)),
        in_specs=[SMEM, VMEM, VMEM],
        out_specs=(VMEM, ANY),
        scratch_shapes=[pltpu.VMEM((PAY, 128), BF16), pltpu.SemaphoreType.DMA((16,))],
        compiler_params=params(FRONT_MIB),
        name="front",
    )(cluster_rows, probes, col_basis)

    def near_product(split, field):
        partner = send(field, CORE)
        other = send(field, SIDE)
        out_shape = [shape((OWN, 32, 128))]
        scratch = [
            pltpu.VMEM((3 * OWN, 64 if split else 32, 256), BF16),
            pltpu.VMEM((OWN, KMAX, 2, 128, 128), BF16),
            pltpu.SemaphoreType.DMA((len(PIECES),)),
        ]
        arguments = [field, partner, other, near_blocks]
        in_specs = [VMEM, VMEM, VMEM, HBM]
        if split:
            out_shape += [shape((OWN, 128, 1024), BF16), shape((OWN, FMAX), jnp.int32)]
            scratch += [
                pltpu.VMEM((OWN, FMAX, 2, RANK, RANK), F32),
                pltpu.SemaphoreType.DMA((len(PACK_PIECES),)),
            ]
            arguments = [far_list] + arguments + [far_coupling]
            in_specs = [VMEM] + in_specs + [HBM]
        return pl.pallas_call(
            functools.partial(near_kernel, split),
            out_shape=out_shape,
            in_specs=[SMEM, SMEM] + in_specs,
            out_specs=[VMEM] * len(out_shape),
            scratch_shapes=scratch,
            compiler_params=params(NEAR_MIB),
            cost_estimate=pl.CostEstimate(
                flops=OWN * KMAX * 8 * 128 * 128 * 16,
                bytes_accessed=OWN * KMAX << 16,
                transcendentals=0,
            ),
            name="near",
        )(near_list, near_count, *arguments)

    near, packed, far_at = near_product(True, base)
    mine, other = gather_all(spread)
    scratch = [pltpu.VMEM((64, RANK, 128), BF16), pltpu.VMEM((4, RANK, 128), BF16)]
    image, narrow, spread, keep = pl.pallas_call(
        image_kernel,
        out_shape=(
            shape((OWN, 32, 128)),
            shape((OWN, 32, 128), BF16),
            shape((16, PAY, 128), BF16),
            shape((PROBES, 128)),
        ),
        in_specs=[SMEM, SMEM] + [VMEM] * 7,
        out_specs=(VMEM, VMEM, ANY, VMEM),
        scratch_shapes=scratch + [pltpu.VMEM((PAY, 128), BF16), pltpu.SemaphoreType.DMA((16,))],
        compiler_params=params(10),
        name="image",
    )(far_at, cluster_rows, mine, other, packed, row_basis, col_basis, near, base)

    (near,) = near_product(False, narrow)
    mine, other = gather_all(spread)
    sums, head = pl.pallas_call(
        inner_kernel,
        out_shape=(shape((PROBES, 128)), shape((PROBES, 128))),
        in_specs=[SMEM, SMEM] + [VMEM] * 8,
        out_specs=(VMEM, VMEM),
        scratch_shapes=scratch,
        compiler_params=params(10),
        name="inner",
    )(far_at, cluster_rows, mine, other, packed, row_basis, near, base, image, keep)

    spread = jnp.broadcast_to(sums[None], (32, PROBES, 128))
    return pl.pallas_call(
        final_kernel,
        out_shape=(shape((OWN, 2, PROBES, 128)), shape((2, PROBES, PROBES)), shape((4, PROBES))),
        in_specs=[SMEM] + [VMEM] * 4,
        out_specs=(VMEM,) * 3,
        compiler_params=params(4),
        name="final",
    )(weight, lax.all_to_all(spread, "clus", 0, 0), head, base, image)


def solution(mesh):
    in_specs = (
        P("clus", None, None, None),
        P(("contour", "clus"), None, None, None, None),
        P("clus", None),
        P("clus"),
        P("clus"),
        P(("contour", "clus"), None, None, None),
        P(("contour", "clus"), None, None, None),
        P("clus", None),
        P(("contour", "clus"), None, None, None, None),
        P("contour"),
    )
    out_specs = (
        P(("contour", "clus"), None, None, None),
        P("contour", None, None),
        P("contour", None),
    )
    return jax.shard_map(shards, mesh=mesh, in_specs=in_specs, out_specs=out_specs, check_vma=False)
```

```python
import functools

import jax
import jax.numpy as jnp
from jax import lax
from jax.experimental import pallas as pl
from jax.experimental.pallas import tpu as pltpu
from jax.sharding import PartitionSpec as P


F32 = jnp.float32
BF16 = jnp.bfloat16
OWN = 8
RANK = 32
PROBES = 16
FMAX = 32
KMAX = 27
FRONT_MIB = 2
DEPTH = 3
PIECES = ((0, 2), (2, 2), (4, 2), (6, 2))
PACK_PIECES = ((0, 4), (4, 4))
NEAR_MIB = 47
STAT = 64
PAY = 80
VMEM = pl.BlockSpec(memory_space=pltpu.VMEM)
SMEM = pl.BlockSpec(memory_space=pltpu.SMEM)
HBM = pl.BlockSpec(memory_space=pltpu.HBM)
ANY = pl.BlockSpec(memory_space=pl.ANY)


def dot_nt(left, right):
    return lax.dot_general(left, right, (((1,), (1,)), ((), ())), preferred_element_type=F32)


def dot_nn(left, right):
    return lax.dot_general(left, right, (((1,), (0,)), ((), ())), preferred_element_type=F32)


def dot_tn(left, right):
    return lax.dot_general(left, right, (((0,), (0,)), ((), ())), preferred_element_type=F32)


def lanes(rows):
    return lax.broadcasted_iota(jnp.int32, (rows, 128), 1)


def paired(field):
    re, im = field[:PROBES], field[PROBES:]
    return jnp.concatenate(
        [jnp.concatenate([re, -im], axis=1), jnp.concatenate([im, re], axis=1)], axis=0
    )


def high_low(value):
    high = value.astype(BF16)
    return high, (value - high.astype(F32)).astype(BF16)


def coefficients(pair, basis):
    both = jnp.concatenate([basis[0], basis[1]], axis=1)
    return dot_nt(both, jnp.concatenate([pair] * 4, axis=0))


def side_by_side(wide):
    block = lanes(RANK) // RANK
    return jnp.where(
        block < 2,
        jnp.where(block == 0, wide[0], wide[1]),
        jnp.where(block == 2, wide[2], wide[3]),
    )


def three_way(column, at):
    lane = lanes(PROBES)
    value = jnp.broadcast_to(column, (PROBES, 128))
    high = value.astype(BF16).astype(F32)
    rest = value - high
    mid = rest.astype(BF16).astype(F32)
    low = rest - mid
    zero = jnp.zeros((PROBES, 128), F32)
    return jnp.where(
        lane == at, high, jnp.where(lane == 32 + at, mid, jnp.where(lane == 64 + at, low, zero))
    )


def column_of(tile, *at):
    lane = lanes(PROBES)
    keep = lane == at[0]
    for a in at[1:]:
        keep = keep | (lane == a)
    return jnp.sum(jnp.where(keep, tile, 0.0), axis=1, keepdims=True)


def gathered_stat(mine, other):
    total = jnp.zeros((PROBES, 128), F32)
    for ref in (mine, other):
        for slot in range(16):
            total = total + ref[slot, STAT:PAY].astype(F32)
    return total


def lane_sum(value):
    return jnp.sum(value, axis=1, keepdims=True)


def twice(column):
    return jnp.concatenate([column, column], axis=0)


def spread_out(pay, spread, sems):
    copies = [
        pltpu.make_async_copy(pay, spread.at[n], sems.at[n]) for n in range(spread.shape[0])
    ]
    for copy in copies:
        copy.start()
    for copy in copies:
        copy.wait()


def front_kernel(rows, probes, col_basis, base, spread, pay, out_sems):
    lane = lanes(2 * PROBES)
    acc = jnp.zeros((PROBES, 128), F32)
    fields = []
    for i in range(OWN):
        raw = jnp.concatenate([probes[i, 0], probes[i, 1]], axis=0)
        field = jnp.where(lane < rows[i], raw, 0.0)
        base[i] = field
        fields.append(field)
        square = field * field
        acc = acc + square[:PROBES] + square[PROBES:]
    wide = []
    for i in range(OWN):
        high, low = high_low(paired(fields[i]))
        basis = col_basis[i]
        wide.append(coefficients(high, basis) + coefficients(low, basis))
    pay[0:32] = side_by_side(wide[:4]).astype(BF16)
    pay[32:64] = side_by_side(wide[4:]).astype(BF16)
    pay[STAT:PAY] = three_way(lane_sum(acc), 0).astype(BF16)
    spread_out(pay, spread, out_sems)


def pack_one(coupling, packed, i):
    for g in range(FMAX // 4):
        four = [coupling[i, 4 * g + f].reshape(2 * RANK, RANK) for f in range(4)]
        high, low = high_low(jnp.concatenate(four, axis=1))
        packed[i, :, 128 * g : 128 * g + 128] = jnp.concatenate([high, low], axis=0)


def near_kernel(split, near_list, near_count, *refs):
    if split:
        far_list, own, partner, other, blocks, coupling, near, packed, far_at = refs[:9]
        table, held, sems, kept, more = refs[9:]
    else:
        own, partner, other, blocks, near, table, held, sems = refs
    pieces = [
        pltpu.make_async_copy(
            blocks.at[pl.ds(at, size)], held.at[pl.ds(at, size)], sems.at[n]
        )
        for n, (at, size) in enumerate(PIECES)
    ]
    for piece in pieces[:DEPTH]:
        piece.start()
    me = lax.axis_index("clus")
    flip = (me & 1) * OWN
    if split:
        late = [
            pltpu.make_async_copy(
                coupling.at[pl.ds(at, size)], kept.at[pl.ds(at, size)], more.at[n]
            )
            for n, (at, size) in enumerate(PACK_PIECES)
        ]
        far = far_list[...]
        owner = far >> 3
        far_at[...] = (((me ^ owner) & 1) * 16 + (owner >> 1)) * OWN + (far & 7)

    def place(i, k):
        local = near_list[i, k] - me * OWN
        return jnp.where(
            local < 0, local + 3 * OWN - flip, jnp.where(local < OWN, local, local + flip)
        )

    for group, ref in enumerate((own, partner, other)):
        for i in range(OWN):
            field = ref[i].astype(F32)
            if split:
                high, low = high_low(paired(field))
                table[OWN * group + i] = jnp.concatenate([high, low], axis=0)
            else:
                table[OWN * group + i] = paired(field).astype(BF16)
    queue = pieces + (late if split else [])
    for n, ((at, size), piece) in enumerate(zip(PIECES, pieces)):
        piece.wait()
        if n + DEPTH < len(queue):
            queue[n + DEPTH].start()
        acc = [jnp.zeros((128, table.shape[1]), F32) for _ in range(size)]
        for k in range(KMAX):
            for j in range(size):
                vec = table[place(at + j, k)]
                vec = jnp.where(k < near_count[at + j], vec, jnp.zeros_like(vec))
                mat = jnp.concatenate([held[at + j, k, 0], held[at + j, k, 1]], axis=1)
                acc[j] = acc[j] + dot_nt(mat, vec)
        for j in range(size):
            out = jnp.transpose(acc[j])
            near[at + j] = out[:32] + out[32:] if split else out
    if split:
        for n, ((at, size), piece) in enumerate(zip(PACK_PIECES, late)):
            piece.wait()
            if len(pieces) + n + DEPTH < len(queue):
                queue[len(pieces) + n + DEPTH].start()
            for i in range(at, at + size):
                pack_one(kept, packed, i)


def far_fields(far_at, mine, other, packed, row_basis, table, masks):
    for half, ref in enumerate((mine, other)):
        for slot in range(16):
            at = 2 * (16 * half + slot)
            table[at : at + 2] = ref[slot, 0:STAT].reshape(2, RANK, 128)
    block = lanes(RANK) // RANK
    for b in range(4):
        masks[b] = jnp.where(block == b, 1.0, 0.0).astype(BF16)
    folded = []
    for i in range(OWN):
        rows = []
        for f in range(FMAX):
            at = far_at[i, f]
            rows.append(table[at >> 2] * masks[at & 3])
        acc = dot_nn(packed[i], jnp.concatenate(rows, axis=0))
        folded.append(acc[:64] + acc[64:])
    both = jnp.concatenate(folded, axis=0)
    both = both + pltpu.roll(both, 64, 1)
    both = both + pltpu.roll(both, 32, 1)
    both = both.reshape(OWN, 2, RANK, 128)
    real, imag = (both[:, c].reshape(OWN * RANK, 128) for c in range(2))
    lane = lanes(OWN * RANK)
    sign = jnp.where((lane // PROBES) % 2 == 0, -1.0, 1.0)
    farcoef = real + sign * pltpu.roll(imag, PROBES, 1)
    turned = sign * pltpu.roll(farcoef, PROBES, 1)
    chosen = []
    for value in (farcoef, turned):
        high = value.astype(BF16).astype(F32)
        chosen.append(jnp.where(lane < 32, high, value - high).astype(BF16))
    out = []
    for i in range(OWN):
        span = slice(RANK * i, RANK * i + RANK)
        left = jnp.concatenate([chosen[0][span], chosen[1][span]], axis=0)
        out.append(dot_tn(left, row_basis[i].reshape(2 * RANK, 128)))
    return [x[0:32] + x[32:64] for x in out]


def image_kernel(far_at, rows, mine, other, *refs):
    packed, row_basis, col_basis, near, base, image, narrow, spread, keep = refs[:-4]
    table, masks, pay, out_sems = refs[-4:]
    far = far_fields(far_at, mine, other, packed, row_basis, table, masks)
    beta = jnp.sqrt(column_of(gathered_stat(mine, other), 0, 32, 64) + 1e-06)
    inverse = twice(1.0 / beta)
    lane = lanes(2 * PROBES)
    acc_re = jnp.zeros((PROBES, 128), F32)
    acc_im = jnp.zeros((PROBES, 128), F32)
    values = []
    for i in range(OWN):
        value = jnp.where(lane < rows[i], near[i] + far[i], 0.0) * inverse
        values.append(value)
        image[i] = value
        narrow[i] = value.astype(BF16)
    wide = [coefficients(paired(values[i]).astype(BF16), col_basis[i]) for i in range(OWN)]
    for i in range(OWN):
        first = base[i] * inverse
        vr, vi = first[:PROBES], first[PROBES:]
        wr, wi = values[i][:PROBES], values[i][PROBES:]
        acc_re = acc_re + vr * wr + vi * wi
        acc_im = acc_im + vr * wi - vi * wr
    pay[0:32] = side_by_side(wide[:4]).astype(BF16)
    pay[32:64] = side_by_side(wide[4:]).astype(BF16)
    pay[STAT:PAY] = (three_way(lane_sum(acc_re), 0) + three_way(lane_sum(acc_im), 1)).astype(BF16)
    keep[...] = jnp.broadcast_to(beta, (PROBES, 128))
    spread_out(pay, spread, out_sems)


def inner_kernel(far_at, rows, mine, other, *refs):
    packed, row_basis, near, base, image, keep, spread, head, table, masks, sums, out_sems = refs
    far = far_fields(far_at, mine, other, packed, row_basis, table, masks)
    stat = gathered_stat(mine, other)
    hr = column_of(stat, 0, 32, 64)
    hi = column_of(stat, 1, 33, 65)
    beta = column_of(keep[...], 0)
    inverse = twice(1.0 / beta)
    lane = lanes(2 * PROBES)

    def times_h(field):
        re, im = field[:PROBES], field[PROBES:]
        return jnp.concatenate([hr * re - hi * im, hr * im + hi * re], axis=0)

    acc = [jnp.zeros((PROBES, 128), F32) for _ in range(9)]
    left, right = [], []
    for i in range(OWN):
        second = jnp.where(lane < rows[i], near[i] + far[i], 0.0)
        w = image[i]
        b = base[i]
        v = b * inverse
        t = w - times_h(v)
        u = second - times_h(w)
        wr, wi, ur, ui = w[:PROBES], w[PROBES:], u[:PROBES], u[PROBES:]
        br, bi, tr, ti = b[:PROBES], b[PROBES:], t[:PROBES], t[PROBES:]
        vr, vi = v[:PROBES], v[PROBES:]
        terms = (
            tr * tr + ti * ti,
            wr * ur + wi * ui,
            wr * ui - wi * ur,
            ur * ur + ui * ui,
            ur * br + ui * bi,
            ur * bi - ui * br,
            wr * wr + wi * wi,
            wr * br + wi * bi,
            wr * bi - wi * br,
        )
        acc = [a + x for a, x in zip(acc, terms)]
        left.append(
            jnp.concatenate(
                [jnp.concatenate([vr, vi], axis=1), jnp.concatenate([tr, ti], axis=1)], axis=0
            )
        )
        right.append(
            jnp.concatenate(
                [jnp.concatenate([br, bi], axis=1), jnp.concatenate([-bi, br], axis=1)], axis=0
            )
        )
    mom = lax.dot_general(
        jnp.concatenate(left, axis=1),
        jnp.concatenate(right, axis=1),
        (((1,), (1,)), ((), ())),
        precision=lax.Precision.HIGHEST,
        preferred_element_type=F32,
    )
    short = lanes(PROBES)
    wide = jnp.concatenate([mom, jnp.zeros((2 * PROBES, 96), F32)], axis=1)
    tile = jnp.where(
        (short >= 16) & (short < 48), pltpu.roll(wide[:PROBES], 16, 1), 0.0
    ) + jnp.where((short >= 48) & (short < 80), pltpu.roll(wide[PROBES:], 48, 1), 0.0)
    for k, term in enumerate(acc):
        tile = tile + jnp.where(short == k, lane_sum(term), 0.0)
    sums[...] = tile
    head[...] = jnp.where(short == 0, beta, jnp.where(short == 1, hr, jnp.where(short == 2, hi, 0.0)))
    spread_out(sums, spread, out_sems)


def prepare_kernel(head, base, image, first, rest):
    beta, hr, hi = (column_of(head[...], k) for k in range(3))
    inverse = 1.0 / beta
    for i in range(OWN):
        vr, vi = base[i, :PROBES] * inverse, base[i, PROBES:] * inverse
        first[i, :PROBES] = vr
        first[i, PROBES:] = vi
        rest[i, :PROBES] = image[i, :PROBES] - (hr * vr - hi * vi)
        rest[i, PROBES:] = image[i, PROBES:] - (hr * vi + hi * vr)


def final_kernel(weight, mine, other, head, first, rest, solution, moment, arnoldi):
    tile = mine[0] + other[0]
    for slot in range(1, mine.shape[0]):
        tile = tile + (mine[slot] + other[slot])
    top = head[...]
    beta, hr, hi = (column_of(top, k) for k in range(3))
    t2, g12r, g12i, g22, q2r, q2i, g11, q1r, q1i = (column_of(tile, k) for k in range(9))
    size = jnp.sqrt(t2 + 1e-06)
    inv = 1.0 / size
    g12r, g12i, q2r, q2i = g12r * inv, g12i * inv, q2r * inv, q2i * inv
    g22 = g22 * inv * inv
    det = g11 * g22 - (g12r * g12r + g12i * g12i)
    y1r = (g22 * q1r - (g12r * q2r - g12i * q2i)) / det
    y1i = (g22 * q1i - (g12r * q2i + g12i * q2r)) / det
    y2r = (g11 * q2r - (g12r * q1r + g12i * q1i)) / det * inv
    y2i = (g11 * q2i - (g12r * q1i - g12i * q1r)) / det * inv
    wr, wi = weight[0], weight[1]
    factor = 1.0 / (256 * 128)
    for i in range(OWN):
        vr, vi = first[i, :PROBES], first[i, PROBES:]
        tr, ti = rest[i, :PROBES], rest[i, PROBES:]
        xr = (y1r * vr - y1i * vi) + (y2r * tr - y2i * ti)
        xi = (y1r * vi + y1i * vr) + (y2r * ti + y2i * tr)
        solution[i, 0] = wr * xr - wi * xi
        solution[i, 1] = wr * xi + wi * xr
    lane = lanes(PROBES)
    sign = jnp.where(lane < 32, -1.0, 1.0)

    def turned(x):
        return sign * jnp.where(lane < 32, pltpu.roll(x, 112, 1), pltpu.roll(x, 16, 1))

    late = pltpu.roll(tile, 96, 1)
    mom = (y1r * tile + y1i * turned(tile)) + (y2r * late + y2i * turned(late))
    mom = (wr * mom + wi * turned(mom)) * factor
    root = jnp.sqrt(jnp.full((1, 1), factor, F32))
    out = jnp.where((lane >= 16) & (lane < 48), mom, 0.0)
    for k, column in enumerate((beta * root, hr, hi, size)):
        out = jnp.where(lane == k, column, out)
    turned_out = jnp.transpose(out)
    moment[0] = turned_out[16:32]
    moment[1] = turned_out[32:48]
    arnoldi[...] = turned_out[0:4]


def shape(dims, dtype=F32):
    return jax.ShapeDtypeStruct(dims, dtype)


def params(mib):
    return pltpu.CompilerParams(vmem_limit_bytes=mib << 20)


CORE = [(i, i ^ 1) for i in range(32)]
SIDE = [(i, (i + 1 if i % 2 else i - 1) % 32) for i in range(32)]
COLUMNS = [list(range(k, 32, 2)) for k in range(2)]


def send(x, pairs):
    return lax.ppermute(x, "clus", pairs)


def gather_all(copies):
    mine = lax.all_to_all(copies, "clus", 0, 0, axis_index_groups=COLUMNS)
    return mine, send(mine, CORE)


def shards(
    probes,
    near_blocks,
    near_list,
    near_count,
    cluster_rows,
    row_basis,
    col_basis,
    far_list,
    far_coupling,
    weight,
):
    base, spread = pl.pallas_call(
        front_kernel,
        out_shape=(shape((OWN, 32, 128)), shape((16, PAY, 128), BF16)),
        in_specs=[SMEM, VMEM, VMEM],
        out_specs=(VMEM, ANY),
        scratch_shapes=[pltpu.VMEM((PAY, 128), BF16), pltpu.SemaphoreType.DMA((16,))],
        compiler_params=params(FRONT_MIB),
        name="front",
    )(cluster_rows, probes, col_basis)

    def near_product(split, field):
        partner = send(field, CORE)
        other = send(field, SIDE)
        out_shape = [shape((OWN, 32, 128))]
        scratch = [
            pltpu.VMEM((3 * OWN, 64 if split else 32, 256), BF16),
            pltpu.VMEM((OWN, KMAX, 2, 128, 128), BF16),
            pltpu.SemaphoreType.DMA((len(PIECES),)),
        ]
        arguments = [field, partner, other, near_blocks]
        in_specs = [VMEM, VMEM, VMEM, HBM]
        if split:
            out_shape += [shape((OWN, 128, 1024), BF16), shape((OWN, FMAX), jnp.int32)]
            scratch += [
                pltpu.VMEM((OWN, FMAX, 2, RANK, RANK), F32),
                pltpu.SemaphoreType.DMA((len(PACK_PIECES),)),
            ]
            arguments = [far_list] + arguments + [far_coupling]
            in_specs = [VMEM] + in_specs + [HBM]
        return pl.pallas_call(
            functools.partial(near_kernel, split),
            out_shape=out_shape,
            in_specs=[SMEM, SMEM] + in_specs,
            out_specs=[VMEM] * len(out_shape),
            scratch_shapes=scratch,
            compiler_params=params(NEAR_MIB),
            cost_estimate=pl.CostEstimate(
                flops=OWN * KMAX * 8 * 128 * 128 * 16,
                bytes_accessed=OWN * KMAX << 16,
                transcendentals=0,
            ),
            name="near",
        )(near_list, near_count, *arguments)

    near, packed, far_at = near_product(True, base)
    mine, other = gather_all(spread)
    scratch = [pltpu.VMEM((64, RANK, 128), BF16), pltpu.VMEM((4, RANK, 128), BF16)]
    image, narrow, spread, keep = pl.pallas_call(
        image_kernel,
        out_shape=(
            shape((OWN, 32, 128)),
            shape((OWN, 32, 128), BF16),
            shape((16, PAY, 128), BF16),
            shape((PROBES, 128)),
        ),
        in_specs=[SMEM, SMEM] + [VMEM] * 7,
        out_specs=(VMEM, VMEM, ANY, VMEM),
        scratch_shapes=scratch + [pltpu.VMEM((PAY, 128), BF16), pltpu.SemaphoreType.DMA((16,))],
        compiler_params=params(10),
        name="image",
    )(far_at, cluster_rows, mine, other, packed, row_basis, col_basis, near, base)

    (near,) = near_product(False, narrow)
    mine, other = gather_all(spread)
    spread, head = pl.pallas_call(
        inner_kernel,
        out_shape=(shape((16, PROBES, 128)), shape((PROBES, 128))),
        in_specs=[SMEM, SMEM] + [VMEM] * 8,
        out_specs=(ANY, VMEM),
        scratch_shapes=scratch + [pltpu.VMEM((PROBES, 128), F32), pltpu.SemaphoreType.DMA((16,))],
        compiler_params=params(10),
        name="inner",
    )(far_at, cluster_rows, mine, other, packed, row_basis, near, base, image, keep)

    field = shape((OWN, 32, 128))
    first, rest = pl.pallas_call(
        prepare_kernel,
        out_shape=(field, field),
        in_specs=[VMEM] * 3,
        out_specs=(VMEM,) * 2,
        compiler_params=params(4),
        cost_estimate=pl.CostEstimate(flops=1 << 20, bytes_accessed=1 << 20, transcendentals=0),
        name="prepare",
    )(head, base, image)
    mine, other = gather_all(spread)
    return pl.pallas_call(
        final_kernel,
        out_shape=(shape((OWN, 2, PROBES, 128)), shape((2, PROBES, PROBES)), shape((4, PROBES))),
        in_specs=[SMEM] + [VMEM] * 5,
        out_specs=(VMEM,) * 3,
        compiler_params=params(4),
        name="final",
    )(weight, mine, other, head, first, rest)


def solution(mesh):
    in_specs = (
        P("clus", None, None, None),
        P(("contour", "clus"), None, None, None, None),
        P("clus", None),
        P("clus"),
        P("clus"),
        P(("contour", "clus"), None, None, None),
        P(("contour", "clus"), None, None, None),
        P("clus", None),
        P(("contour", "clus"), None, None, None, None),
        P("contour"),
    )
    out_specs = (
        P(("contour", "clus"), None, None, None),
        P("contour", None, None),
        P("contour", None),
    )
    return jax.shard_map(shards, mesh=mesh, in_specs=in_specs, out_specs=out_specs, check_vma=False)
```

```python
import functools

import jax
import jax.numpy as jnp
from jax import lax
from jax.experimental import pallas as pl
from jax.experimental.pallas import tpu as pltpu
from jax.sharding import PartitionSpec as P


F32 = jnp.float32
BF16 = jnp.bfloat16
OWN = 8
RANK = 32
PROBES = 16
FMAX = 32
KMAX = 27
FRONT_MIB = 2
DEPTH = 3
PIECES = ((0, 2), (2, 2), (4, 2), (6, 2))
PACK_PIECES = ((0, 4), (4, 4))
NEAR_MIB = 47
STAT = 64
PAY = 80
VMEM = pl.BlockSpec(memory_space=pltpu.VMEM)
SMEM = pl.BlockSpec(memory_space=pltpu.SMEM)
HBM = pl.BlockSpec(memory_space=pltpu.HBM)


def dot_nt(left, right):
    return lax.dot_general(left, right, (((1,), (1,)), ((), ())), preferred_element_type=F32)


def dot_nn(left, right):
    return lax.dot_general(left, right, (((1,), (0,)), ((), ())), preferred_element_type=F32)


def dot_tn(left, right):
    return lax.dot_general(left, right, (((0,), (0,)), ((), ())), preferred_element_type=F32)


def lanes(rows):
    return lax.broadcasted_iota(jnp.int32, (rows, 128), 1)


def paired(field):
    re, im = field[:PROBES], field[PROBES:]
    return jnp.concatenate(
        [jnp.concatenate([re, -im], axis=1), jnp.concatenate([im, re], axis=1)], axis=0
    )


def high_low(value):
    high = value.astype(BF16)
    return high, (value - high.astype(F32)).astype(BF16)


def coefficients(pair, basis):
    both = jnp.concatenate([basis[0], basis[1]], axis=1)
    return dot_nt(both, jnp.concatenate([pair] * 4, axis=0))


def side_by_side(wide):
    block = lanes(RANK) // RANK
    return jnp.where(
        block < 2,
        jnp.where(block == 0, wide[0], wide[1]),
        jnp.where(block == 2, wide[2], wide[3]),
    )


def three_way(column, at):
    lane = lanes(PROBES)
    value = jnp.broadcast_to(column, (PROBES, 128))
    high = value.astype(BF16).astype(F32)
    rest = value - high
    mid = rest.astype(BF16).astype(F32)
    low = rest - mid
    zero = jnp.zeros((PROBES, 128), F32)
    return jnp.where(
        lane == at, high, jnp.where(lane == 32 + at, mid, jnp.where(lane == 64 + at, low, zero))
    )


def column_of(tile, *at):
    lane = lanes(PROBES)
    keep = lane == at[0]
    for a in at[1:]:
        keep = keep | (lane == a)
    return jnp.sum(jnp.where(keep, tile, 0.0), axis=1, keepdims=True)


def gathered_stat(*parts):
    total = jnp.zeros((PROBES, 128), F32)
    for part in parts:
        for slot in range(part.shape[0]):
            total = total + part[slot, STAT:PAY].astype(F32)
    return total


def lane_sum(value):
    return jnp.sum(value, axis=1, keepdims=True)


def twice(column):
    return jnp.concatenate([column, column], axis=0)


def spread_out(pay, spread, sems):
    copies = [
        pltpu.make_async_copy(pay, spread.at[n], sems.at[n]) for n in range(spread.shape[0])
    ]
    for copy in copies:
        copy.start()
    for copy in copies:
        copy.wait()


def front_kernel(base, col_basis, spread, pay, out_sems):
    acc = jnp.zeros((PROBES, 128), F32)
    fields = []
    for i in range(OWN):
        field = base[i]
        fields.append(field)
        square = field * field
        acc = acc + square[:PROBES] + square[PROBES:]
    wide = []
    for i in range(OWN):
        high, low = high_low(paired(fields[i]))
        basis = col_basis[i]
        wide.append(coefficients(high, basis) + coefficients(low, basis))
    pay[0:32] = side_by_side(wide[:4]).astype(BF16)
    pay[32:64] = side_by_side(wide[4:]).astype(BF16)
    pay[STAT:PAY] = three_way(lane_sum(acc), 0).astype(BF16)
    spread_out(pay, spread, out_sems)


def pack_one(coupling, packed, i):
    for g in range(FMAX // 4):
        four = [coupling[i, 4 * g + f].reshape(2 * RANK, RANK) for f in range(4)]
        high, low = high_low(jnp.concatenate(four, axis=1))
        packed[i, :, 128 * g : 128 * g + 128] = jnp.concatenate([high, low], axis=0)


def near_kernel(split, meta, *refs):
    if split:
        own, partner, other, blocks, coupling, near, packed = refs[:7]
        table, held, sems, kept, more = refs[7:]
    else:
        own, partner, other, blocks, near, table, held, sems = refs
    pieces = [
        pltpu.make_async_copy(
            blocks.at[pl.ds(at, size)], held.at[pl.ds(at, size)], sems.at[n]
        )
        for n, (at, size) in enumerate(PIECES)
    ]
    for piece in pieces[:DEPTH]:
        piece.start()
    me = lax.axis_index("clus")
    flip = (me & 1) * OWN
    if split:
        late = [
            pltpu.make_async_copy(
                coupling.at[pl.ds(at, size)], kept.at[pl.ds(at, size)], more.at[n]
            )
            for n, (at, size) in enumerate(PACK_PIECES)
        ]

    def place(i, k):
        local = meta[i, k] - me * OWN
        return jnp.where(
            local < 0, local + 3 * OWN - flip, jnp.where(local < OWN, local, local + flip)
        )

    for group, ref in enumerate((own, partner, other)):
        for i in range(OWN):
            field = ref[i].astype(F32)
            if split:
                high, low = high_low(paired(field))
                table[OWN * group + i] = jnp.concatenate([high, low], axis=0)
            else:
                table[OWN * group + i] = paired(field).astype(BF16)
    queue = pieces + (late if split else [])
    for n, ((at, size), piece) in enumerate(zip(PIECES, pieces)):
        piece.wait()
        if n + DEPTH < len(queue):
            queue[n + DEPTH].start()
        acc = [jnp.zeros((128, table.shape[1]), F32) for _ in range(size)]
        for k in range(KMAX):
            for j in range(size):
                vec = table[place(at + j, k)]
                vec = jnp.where(k < meta[OWN, at + j], vec, jnp.zeros_like(vec))
                mat = jnp.concatenate([held[at + j, k, 0], held[at + j, k, 1]], axis=1)
                acc[j] = acc[j] + dot_nt(mat, vec)
        for j in range(size):
            out = jnp.transpose(acc[j])
            near[at + j] = out[:32] + out[32:] if split else out
    if split:
        for n, ((at, size), piece) in enumerate(zip(PACK_PIECES, late)):
            piece.wait()
            if len(pieces) + n + DEPTH < len(queue):
                queue[len(pieces) + n + DEPTH].start()
            for i in range(at, at + size):
                pack_one(kept, packed, i)


def far_fields(far_list, parts, packed, row_basis, table, masks):
    parity = lax.axis_index("clus") & 1
    for half, part in enumerate(parts):
        for slot in range(part.shape[0]):
            owner = slot if len(parts) == 1 else 2 * slot + (parity ^ half)
            table[pl.ds(2 * owner, 2)] = part[slot, 0:STAT].reshape(2, RANK, 128)
    block = lanes(RANK) // RANK
    for b in range(4):
        masks[b] = jnp.where(block == b, 1.0, 0.0).astype(BF16)
    folded = []
    for i in range(OWN):
        rows = []
        for f in range(FMAX):
            at = far_list[i, f]
            rows.append(table[at >> 2] * masks[at & 3])
        acc = dot_nn(packed[i], jnp.concatenate(rows, axis=0))
        folded.append(acc[:64] + acc[64:])
    both = jnp.concatenate(folded, axis=0)
    both = both + pltpu.roll(both, 64, 1)
    both = both + pltpu.roll(both, 32, 1)
    both = both.reshape(OWN, 2, RANK, 128)
    real, imag = (both[:, c].reshape(OWN * RANK, 128) for c in range(2))
    lane = lanes(OWN * RANK)
    sign = jnp.where((lane // PROBES) % 2 == 0, -1.0, 1.0)
    farcoef = real + sign * pltpu.roll(imag, PROBES, 1)
    turned = sign * pltpu.roll(farcoef, PROBES, 1)
    chosen = []
    for value in (farcoef, turned):
        high = value.astype(BF16).astype(F32)
        chosen.append(jnp.where(lane < 32, high, value - high).astype(BF16))
    out = []
    for i in range(OWN):
        span = slice(RANK * i, RANK * i + RANK)
        left = jnp.concatenate([chosen[0][span], chosen[1][span]], axis=0)
        out.append(dot_tn(left, row_basis[i].reshape(2 * RANK, 128)))
    return [x[0:32] + x[32:64] for x in out]


def image_kernel(far_list, rows, whole, *refs):
    packed, row_basis, col_basis, near, base, image, narrow, spread = refs[:-4]
    table, masks, pay, out_sems = refs[-4:]
    far = far_fields(far_list, (whole,), packed, row_basis, table, masks)
    beta = jnp.sqrt(column_of(gathered_stat(whole), 0, 32, 64) + 1e-06)
    inverse = twice(1.0 / beta)
    lane = lanes(2 * PROBES)
    acc_re = jnp.zeros((PROBES, 128), F32)
    acc_im = jnp.zeros((PROBES, 128), F32)
    acc_sq = jnp.zeros((PROBES, 128), F32)
    values = []
    for i in range(OWN):
        value = jnp.where(lane < rows[i], near[i] + far[i], 0.0) * inverse
        values.append(value)
        image[i] = value
        narrow[i] = value.astype(BF16)
    wide = [coefficients(paired(values[i]).astype(BF16), col_basis[i]) for i in range(OWN)]
    for i in range(OWN):
        first = base[i] * inverse
        vr, vi = first[:PROBES], first[PROBES:]
        wr, wi = values[i][:PROBES], values[i][PROBES:]
        acc_re = acc_re + vr * wr + vi * wi
        acc_im = acc_im + vr * wi - vi * wr
        square = base[i] * base[i]
        acc_sq = acc_sq + square[:PROBES] + square[PROBES:]
    pay[0:32] = side_by_side(wide[:4]).astype(BF16)
    pay[32:64] = side_by_side(wide[4:]).astype(BF16)
    stats = (acc_re, acc_im, acc_sq)
    pay[STAT:PAY] = sum(three_way(lane_sum(x), n) for n, x in enumerate(stats)).astype(BF16)
    spread_out(pay, spread, out_sems)


def inner_kernel(far_list, rows, mine, other, *refs):
    packed, row_basis, near, base, image, spread, head, table, masks, sums, out_sems = refs
    far = far_fields(far_list, (mine, other), packed, row_basis, table, masks)
    stat = gathered_stat(mine, other)
    hr = column_of(stat, 0, 32, 64)
    hi = column_of(stat, 1, 33, 65)
    beta = jnp.sqrt(column_of(stat, 2, 34, 66) + 1e-06)
    inverse = twice(1.0 / beta)
    lane = lanes(2 * PROBES)

    def times_h(field):
        re, im = field[:PROBES], field[PROBES:]
        return jnp.concatenate([hr * re - hi * im, hr * im + hi * re], axis=0)

    acc = [jnp.zeros((PROBES, 128), F32) for _ in range(9)]
    left, right = [], []
    for i in range(OWN):
        second = jnp.where(lane < rows[i], near[i] + far[i], 0.0)
        w = image[i]
        b = base[i]
        v = b * inverse
        t = w - times_h(v)
        u = second - times_h(w)
        wr, wi, ur, ui = w[:PROBES], w[PROBES:], u[:PROBES], u[PROBES:]
        br, bi, tr, ti = b[:PROBES], b[PROBES:], t[:PROBES], t[PROBES:]
        vr, vi = v[:PROBES], v[PROBES:]
        terms = (
            tr * tr + ti * ti,
            wr * ur + wi * ui,
            wr * ui - wi * ur,
            ur * ur + ui * ui,
            ur * br + ui * bi,
            ur * bi - ui * br,
            wr * wr + wi * wi,
            wr * br + wi * bi,
            wr * bi - wi * br,
        )
        acc = [a + x for a, x in zip(acc, terms)]
        left.append(
            jnp.concatenate(
                [jnp.concatenate([vr, vi], axis=1), jnp.concatenate([tr, ti], axis=1)], axis=0
            )
        )
        right.append(
            jnp.concatenate(
                [jnp.concatenate([br, bi], axis=1), jnp.concatenate([-bi, br], axis=1)], axis=0
            )
        )
    mom = lax.dot_general(
        jnp.concatenate(left, axis=1),
        jnp.concatenate(right, axis=1),
        (((1,), (1,)), ((), ())),
        precision=lax.Precision.HIGHEST,
        preferred_element_type=F32,
    )
    short = lanes(PROBES)
    wide = jnp.concatenate([mom, jnp.zeros((2 * PROBES, 96), F32)], axis=1)
    tile = jnp.where(
        (short >= 16) & (short < 48), pltpu.roll(wide[:PROBES], 16, 1), 0.0
    ) + jnp.where((short >= 48) & (short < 80), pltpu.roll(wide[PROBES:], 48, 1), 0.0)
    for k, term in enumerate(acc):
        tile = tile + jnp.where(short == k, lane_sum(term), 0.0)
    sums[...] = tile
    head[...] = jnp.where(short == 0, beta, jnp.where(short == 1, hr, jnp.where(short == 2, hi, 0.0)))
    spread_out(sums, spread, out_sems)


def prepare_kernel(head, base, image, first, rest):
    beta, hr, hi = (column_of(head[...], k) for k in range(3))
    inverse = 1.0 / beta
    for i in range(OWN):
        vr, vi = base[i, :PROBES] * inverse, base[i, PROBES:] * inverse
        first[i, :PROBES] = vr
        first[i, PROBES:] = vi
        rest[i, :PROBES] = image[i, :PROBES] - (hr * vr - hi * vi)
        rest[i, PROBES:] = image[i, PROBES:] - (hr * vi + hi * vr)


def final_kernel(weight, whole, head, first, rest, solution, moment, arnoldi):
    tile = whole[0]
    for slot in range(1, 32):
        tile = tile + whole[slot]
    top = head[...]
    beta, hr, hi = (column_of(top, k) for k in range(3))
    t2, g12r, g12i, g22, q2r, q2i, g11, q1r, q1i = (column_of(tile, k) for k in range(9))
    size = jnp.sqrt(t2 + 1e-06)
    inv = 1.0 / size
    g12r, g12i, q2r, q2i = g12r * inv, g12i * inv, q2r * inv, q2i * inv
    g22 = g22 * inv * inv
    det = g11 * g22 - (g12r * g12r + g12i * g12i)
    y1r = (g22 * q1r - (g12r * q2r - g12i * q2i)) / det
    y1i = (g22 * q1i - (g12r * q2i + g12i * q2r)) / det
    y2r = (g11 * q2r - (g12r * q1r + g12i * q1i)) / det * inv
    y2i = (g11 * q2i - (g12r * q1i - g12i * q1r)) / det * inv
    wr, wi = weight[0], weight[1]
    factor = 1.0 / (256 * 128)
    for i in range(OWN):
        vr, vi = first[i, :PROBES], first[i, PROBES:]
        tr, ti = rest[i, :PROBES], rest[i, PROBES:]
        xr = (y1r * vr - y1i * vi) + (y2r * tr - y2i * ti)
        xi = (y1r * vi + y1i * vr) + (y2r * ti + y2i * tr)
        solution[i, 0] = wr * xr - wi * xi
        solution[i, 1] = wr * xi + wi * xr
    lane = lanes(PROBES)
    sign = jnp.where(lane < 32, -1.0, 1.0)

    def turned(x):
        return sign * jnp.where(lane < 32, pltpu.roll(x, 112, 1), pltpu.roll(x, 16, 1))

    late = pltpu.roll(tile, 96, 1)
    mom = (y1r * tile + y1i * turned(tile)) + (y2r * late + y2i * turned(late))
    mom = (wr * mom + wi * turned(mom)) * factor
    root = jnp.sqrt(jnp.full((1, 1), factor, F32))
    out = jnp.where((lane >= 16) & (lane < 48), mom, 0.0)
    for k, column in enumerate((beta * root, hr, hi, size)):
        out = jnp.where(lane == k, column, out)
    turned_out = jnp.transpose(out)
    moment[0] = turned_out[16:32]
    moment[1] = turned_out[32:48]
    arnoldi[...] = turned_out[0:4]


def shape(dims, dtype=F32):
    return jax.ShapeDtypeStruct(dims, dtype)


def params(mib):
    return pltpu.CompilerParams(vmem_limit_bytes=mib << 20)


CORE = [(i, i ^ 1) for i in range(32)]
COLUMNS = [list(range(k, 32, 2)) for k in range(2)]
SIDE = [(i, (i + 1 if i % 2 else i - 1) % 32) for i in range(32)]


def send(x, pairs):
    return lax.ppermute(x, "clus", pairs)


def gather_all(copies):
    return lax.all_to_all(copies, "clus", 0, 0)


def gather_halves(copies):
    mine = lax.all_to_all(copies, "clus", 0, 0, axis_index_groups=COLUMNS)
    return mine, send(mine, CORE)


def shards(
    probes,
    near_blocks,
    near_list,
    near_count,
    cluster_rows,
    row_basis,
    col_basis,
    far_list,
    far_coupling,
    weight,
):
    rows_iota = lax.broadcasted_iota(jnp.int32, (OWN, 1, 1, 128), 3)
    live = rows_iota < cluster_rows[:, None, None, None]
    base = jnp.where(live, probes, 0.0).reshape(OWN, 32, 128)
    meta = jnp.pad(near_list, ((0, 1), (0, 0))) + jnp.pad(
        near_count[None], ((OWN, 0), (0, KMAX - OWN))
    )

    def front():
        return pl.pallas_call(
            front_kernel,
            out_shape=shape((32, PAY, 128), BF16),
            in_specs=[VMEM, VMEM],
            out_specs=HBM,
            scratch_shapes=[pltpu.VMEM((PAY, 128), BF16), pltpu.SemaphoreType.DMA((32,))],
            compiler_params=params(FRONT_MIB),
            cost_estimate=pl.CostEstimate(flops=1 << 20, bytes_accessed=1 << 20, transcendentals=0),
            name="front",
        )(base, col_basis)

    def near_product(split, field):
        partner = send(field, CORE)
        other = send(field, SIDE)
        out_shape = [shape((OWN, 32, 128))]
        scratch = [
            pltpu.VMEM((3 * OWN, 64 if split else 32, 256), BF16),
            pltpu.VMEM((OWN, KMAX, 2, 128, 128), BF16),
            pltpu.SemaphoreType.DMA((len(PIECES),)),
        ]
        arguments = [field, partner, other, near_blocks]
        in_specs = [VMEM, VMEM, VMEM, HBM]
        if split:
            out_shape += [shape((OWN, 128, 1024), BF16)]
            scratch += [
                pltpu.VMEM((OWN, FMAX, 2, RANK, RANK), F32),
                pltpu.SemaphoreType.DMA((len(PACK_PIECES),)),
            ]
            arguments += [far_coupling]
            in_specs += [HBM]
        return pl.pallas_call(
            functools.partial(near_kernel, split),
            out_shape=out_shape,
            in_specs=[SMEM] + in_specs,
            out_specs=[VMEM] * len(out_shape),
            scratch_shapes=scratch,
            compiler_params=params(NEAR_MIB),
            cost_estimate=pl.CostEstimate(
                flops=OWN * KMAX * 8 * 128 * 128 * 16,
                bytes_accessed=OWN * KMAX << 16,
                transcendentals=0,
            ),
            name="near",
        )(meta, *arguments)

    spread = front()
    near, packed = near_product(True, base)
    whole = gather_all(spread)
    scratch = [pltpu.VMEM((64, RANK, 128), BF16), pltpu.VMEM((4, RANK, 128), BF16)]
    image, narrow, spread = pl.pallas_call(
        image_kernel,
        out_shape=(
            shape((OWN, 32, 128)),
            shape((OWN, 32, 128), BF16),
            shape((16, PAY, 128), BF16),
        ),
        in_specs=[SMEM, SMEM] + [VMEM] * 6,
        out_specs=(VMEM, VMEM, HBM),
        scratch_shapes=scratch + [pltpu.VMEM((PAY, 128), BF16), pltpu.SemaphoreType.DMA((16,))],
        compiler_params=params(10),
        name="image",
    )(far_list, cluster_rows, whole, packed, row_basis, col_basis, near, base)

    (near,) = near_product(False, narrow)
    mine, other = gather_halves(spread)
    spread, head = pl.pallas_call(
        inner_kernel,
        out_shape=(shape((32, PROBES, 128)), shape((PROBES, 128))),
        in_specs=[SMEM, SMEM] + [VMEM] * 7,
        out_specs=(HBM, VMEM),
        scratch_shapes=scratch + [pltpu.VMEM((PROBES, 128), F32), pltpu.SemaphoreType.DMA((32,))],
        compiler_params=params(10),
        name="inner",
    )(far_list, cluster_rows, mine, other, packed, row_basis, near, base, image)

    field = shape((OWN, 32, 128))
    first, rest = pl.pallas_call(
        prepare_kernel,
        out_shape=(field, field),
        in_specs=[VMEM] * 3,
        out_specs=(VMEM,) * 2,
        compiler_params=params(4),
        cost_estimate=pl.CostEstimate(flops=1 << 20, bytes_accessed=1 << 20, transcendentals=0),
        name="prepare",
    )(head, base, image)
    whole = gather_all(spread)
    return pl.pallas_call(
        final_kernel,
        out_shape=(shape((OWN, 2, PROBES, 128)), shape((2, PROBES, PROBES)), shape((4, PROBES))),
        in_specs=[SMEM] + [VMEM] * 4,
        out_specs=(VMEM,) * 3,
        compiler_params=params(4),
        name="final",
    )(weight, whole, head, first, rest)


def solution(mesh):
    in_specs = (
        P("clus", None, None, None),
        P(("contour", "clus"), None, None, None, None),
        P("clus", None),
        P("clus"),
        P("clus"),
        P(("contour", "clus"), None, None, None),
        P(("contour", "clus"), None, None, None),
        P("clus", None),
        P(("contour", "clus"), None, None, None, None),
        P("contour"),
    )
    out_specs = (
        P(("contour", "clus"), None, None, None),
        P("contour", None, None),
        P("contour", None),
    )
    return jax.shard_map(shards, mesh=mesh, in_specs=in_specs, out_specs=out_specs, check_vma=False)
```
